768 devices in a mesh: grp: 8 (over y), slab: 12 (over z_lo, core), row: 8 (over x, z_hi).
Axes of the slice: x: 4, y: 8, z: 12 (z_hi: 2, z_lo: 6; z = z_hi * 6 + z_lo), core: 2. Of those that a mesh axis runs over, the one named last changes fastest.
Arguments:
- velocity: float32 [3, 384, 64, 1024], P(None, 'slab', 'grp', 'row'), may hold values from -6 to 6
- modes: float32 [196608, 512], P(('grp', 'slab', 'row')), may hold values from -6 to 6
- planes: int32 [64], replicated, may hold values from 0 to 383, as said below
- assign: int32 [12], replicated, may hold values from 0 to 11, each once
Outputs:
- advanced: float32 [3, 384, 64, 1024], P(None, 'slab', 'grp', 'row')
- basis: float32 [196608, 576], P(('grp', 'slab', 'row'))
- factor: float32 [576, 576], replicated
The draws below stay inside these ranges and needn't reach their ends.
Inputs may be any that keep to these rules, and one draw needn't show every extreme that they name: `planes`: the 64 plane indices are distinct.
All inputs are finite; a program needn't handle non-finite values.
Results may differ from the reference program's by a relative error of at most 0.00005.
Values sent between devices are 32-bit elements; how exact they have to be, the bound alone decides.
No kernel may reach another device: no remote copies, remote signals or barrier semaphores. Data moves between devices by JAX's collectives and lax.ppermute only.
A program may use at most 32 MiB of HBM per device.

```python
import jax
import jax.numpy as jnp
from jax import lax

CX = 8
CY = 128
NSNAP = 64
RANK = 512
NX = 64
NY = 1024
NZ = 384
BLK = 256
ROWS = 196608
N_GRP = 8
N_SLAB = 12
N_ROW = 8


def draw_planes(key, part):
    keys = jax.random.split(jax.random.fold_in(key, 17), 2)
    others = jnp.concatenate([jnp.arange(NSNAP - 1, dtype=jnp.int32), jnp.arange(NSNAP + 1, 2 * NSNAP, dtype=jnp.int32)])
    chosen = others[jax.random.permutation(keys[0], 2 * NSNAP - 2)[:NSNAP - 2]]
    offsets = jnp.concatenate([chosen, jnp.array([NSNAP - 1, NSNAP], dtype=jnp.int32)])
    offsets = offsets[jax.random.permutation(keys[1], NSNAP)]
    return ((NZ - NSNAP + offsets) % NZ).astype(jnp.int32)


def block_levels(stream_key, extent, pieces, least, high):
    def one(position, blocks):
        steps = jax.random.uniform(jax.random.fold_in(jax.random.fold_in(stream_key, 6), position), (blocks,), jnp.float32, least / len(pieces), high / len(pieces))
        return jnp.repeat(jnp.exp(steps), extent[position] // blocks).reshape((-1,) + (1,) * (len(extent) - position - 1))

    level = one(*pieces[0])
    for cut in pieces[1:]:
        level = level * one(*cut)
    return level


def gaussian(rng, extent, scale, reach, shards=(), kind=jnp.bfloat16):
    values = scale * jax.random.normal(rng, extent, jnp.float32)
    if shards:
        values = values * block_levels(rng, extent, shards, -0.22, 0.18)
    return jnp.clip(values, -reach, reach).astype(kind)


def setup_inputs(seed: int = 0) -> dict:
    arg_keys = jax.random.split(jax.random.key(seed), 5)
    return {
        "velocity": gaussian(arg_keys[0], (3, NZ, NX, NY), 1.0, 6.0, ((1, 12), (2, 8), (3, 8)), jnp.float32),
        "modes": gaussian(arg_keys[1], (ROWS, RANK), 1.0, 6.0, ((0, 768),), jnp.float32),
        "planes": draw_planes(jax.random.fold_in(arg_keys[4], 71), 0),
        "assign": jax.random.permutation(arg_keys[3], N_SLAB).astype(jnp.int32),
    }


step_size = 0.05
viscosity = 1.0
third = 1.0 / 3.0
carry_back = -5.0 / 9.0
second_gain = 15.0 / 16.0

def derivatives(parts):
    first = (parts[0] - 8.0 * parts[1] + 8.0 * parts[3] - parts[4]) / 12.0
    second = (-parts[0] + 16.0 * parts[1] - 30.0 * parts[2] + 16.0 * parts[3] - parts[4]) / 12.0
    return (first, second)

def periodic_parts(field, dim):
    return [jnp.roll(field, 2 - k, axis=dim) for k in range(5)]

def wall_parts(field, dim):
    length = field.shape[dim]
    widths = [(0, 0)] * field.ndim
    widths[dim] = (2, 2)
    padded = jnp.pad(field, widths)
    return [lax.slice_in_dim(padded, k, k + length, axis=dim) for k in range(5)]

def tendency(along_z, along_x, along_y, field):
    dz_first, dz_second = derivatives(along_z)
    dx_first, dx_second = derivatives(along_x)
    dy_first, dy_second = derivatives(along_y)
    convect = field[0:1] * dx_first + field[1:2] * dy_first + field[2:3] * dz_first
    laplace = dx_second + dy_second + dz_second
    return viscosity * laplace - convect

def whole_tendency(field):
    return tendency(periodic_parts(field, 1), periodic_parts(field, 2), wall_parts(field, 3), field)

def reference(velocity, modes, planes, assign):
    first_q = step_size * whole_tendency(velocity)
    middle = velocity + third * first_q
    second_q = carry_back * first_q + step_size * whole_tendency(middle)
    advanced = middle + second_gain * second_q
    picked = jnp.take(advanced, planes, axis=1)
    picked = jnp.transpose(picked, (1, 0, 2, 3)).reshape(NSNAP, 3, N_GRP, CX, N_ROW, CY)
    picked = jnp.transpose(picked, (0, 2, 4, 1, 3, 5)).reshape(NSNAP, N_GRP, N_ROW, N_SLAB, BLK)
    picked = jnp.take(picked, assign, axis=3)
    snapshot_block = jnp.transpose(picked, (1, 3, 2, 4, 0)).reshape(ROWS, NSNAP)
    joined = jnp.concatenate([modes, snapshot_block], axis=1)
    gram = jnp.dot(joined.T.astype(jnp.float32), joined.astype(jnp.float32), precision=lax.Precision.HIGHEST, preferred_element_type=jnp.float32) / float(ROWS)
    lower = jnp.linalg.cholesky(gram)
    basis = jax.scipy.linalg.solve_triangular(lower, joined.T, lower=True).T
    return (advanced, basis, lower.T)
```

```python
import jax
import jax.numpy as jnp
from jax import lax
from jax.experimental import pallas as pl
from jax.experimental.pallas import tpu as pltpu
from jax.sharding import PartitionSpec as P

step_size = 0.05
viscosity = 1.0
third = 1.0 / 3.0
carry_back = -5.0 / 9.0
second_gain = 15.0 / 16.0

ALL = ("grp", "slab", "row")
WIDE = 4
BLOCK = 128
VMEM_LIMIT = 48 * 1024 * 1024


def vmem_call(kernel, out_shape, in_specs, scratch=(), aliases=None, flops=0, moved=0):
    single = not isinstance(out_shape, (list, tuple))
    whole = pl.BlockSpec(memory_space=pltpu.VMEM)
    return pl.pallas_call(
        kernel,
        out_shape=out_shape,
        in_specs=in_specs,
        out_specs=whole if single else [whole] * len(out_shape),
        scratch_shapes=list(scratch),
        input_output_aliases=aliases or {},
        cost_estimate=pl.CostEstimate(flops=flops, bytes_accessed=moved, transcendentals=0),
        compiler_params=pltpu.CompilerParams(vmem_limit_bytes=VMEM_LIMIT),
    )


VM = pl.BlockSpec(memory_space=pltpu.VMEM)
SM = pl.BlockSpec(memory_space=pltpu.SMEM)


def product(left, right, dims):
    return lax.dot_general(
        left,
        right,
        (dims, ((), ())),
        precision=lax.Precision.HIGHEST,
        preferred_element_type=jnp.float32,
    )


def both_ways(low, high, axis, wrap):
    devices = lax.axis_size(axis)
    up = [(i, (i + 1) % devices) for i in range(devices if wrap else devices - 1)]
    down = [(j, i) for i, j in up]
    return lax.ppermute(high, axis, up), lax.ppermute(low, axis, down)


def pack_kernel(field_ref, first_ref, last_ref):
    comps, depth, rows, lanes = field_ref.shape
    planes = comps * depth
    group = lanes // WIDE
    lane = lax.broadcasted_iota(jnp.int32, (rows, lanes), 1)
    for tile in range(first_ref.shape[0]):
        head = jnp.zeros((rows, lanes), jnp.float32)
        tail = jnp.zeros((rows, lanes), jnp.float32)
        for q in range(min(group, planes - tile * group)):
            c, z = divmod(tile * group + q, depth)
            value = field_ref[c, z]
            here = (lane >= WIDE * q) & (lane < WIDE * (q + 1))
            head = jnp.where(here, pltpu.roll(value, (WIDE * q) % lanes, 1), head)
            tail = jnp.where(here, pltpu.roll(value, (WIDE * (q + 1)) % lanes, 1), tail)
        first_ref[tile] = head
        last_ref[tile] = tail


def parts_of(value, axis):
    size = value.shape[axis]
    return [pltpu.roll(value, shift % size, axis) for shift in (2, 1, -1, -2)]


def derivatives(parts, centre):
    far = parts[0], parts[3]
    first = ((far[0] - far[1]) + 8.0 * (parts[2] - parts[1])) * (1.0 / 12.0)
    second = (16.0 * (parts[1] + parts[2]) - (far[0] + far[1]) - 30.0 * centre) * (1.0 / 12.0)
    return first, second


def sections_kernel(
    assign_ref, row_ref, field_ref, before_ref, after_ref, out_ref, sent_ref, wide_ref, mid_ref, q_ref, place_ref
):
    comps, depth_wide, rows, lanes = field_ref.shape
    depth, across = out_ref.shape[1], out_ref.shape[2]
    group = lanes // WIDE
    lane = lax.broadcasted_iota(jnp.int32, (rows, lanes), 1)

    for c in range(comps):
        for z in range(depth_wide):
            tile, q = divmod(c * depth_wide + z, group)
            after = pltpu.roll(after_ref[tile], (-WIDE * q) % lanes, 1)
            before = pltpu.roll(before_ref[tile], (-WIDE * (q + 1)) % lanes, 1)
            halo = jnp.where(lane < WIDE, after, jnp.where(lane >= lanes - WIDE, before, 0.0))
            wide_ref[c, z, :, 0:lanes] = field_ref[c, z]
            wide_ref[c, z, :, lanes : 2 * lanes] = halo

    edge = lax.broadcasted_iota(jnp.int32, (rows, 2 * lanes), 1)
    outside = ((edge >= lanes + lanes // 2) & (row_ref[0] == 0)) | (
        (edge >= lanes) & (edge < lanes + lanes // 2) & (row_ref[0] == row_ref[1] - 1)
    )

    def tendency(speeds, centre, along_z, along_x, along_y):
        dz_first, dz_second = derivatives(along_z, centre)
        dx_first, dx_second = derivatives(along_x, centre)
        dy_first, dy_second = derivatives(along_y, centre)
        convect = speeds[0] * dx_first + speeds[1] * dy_first + speeds[2] * dz_first
        return viscosity * (dx_second + dy_second + dz_second) - convect

    def first_section(z, _):
        speeds = [wide_ref[c, z] for c in range(comps)]
        for c in range(comps):
            along_z = [wide_ref[c, z + k] for k in (-2, -1, 1, 2)]
            slope = tendency(speeds, speeds[c], along_z, parts_of(speeds[c], 0), parts_of(speeds[c], 1))
            q = step_size * slope
            mid_ref[c, z] = jnp.where(outside, 0.0, speeds[c] + third * q)
            q_ref[c, z] = q[:across, :lanes]
        return 0

    lax.fori_loop(2, depth_wide - 2, first_section, 0)

    def second_section(z, _):
        speeds = [mid_ref[c, z, 0:across, 0:lanes] for c in range(comps)]
        for c in range(comps):
            along_z = [mid_ref[c, z + k, 0:across, 0:lanes] for k in (-2, -1, 1, 2)]
            along_x = [p[:across] for p in parts_of(mid_ref[c, z, :, 0:lanes], 0)]
            along_y = [p[:, :lanes] for p in parts_of(mid_ref[c, z, 0:across, :], 1)]
            slope = tendency(speeds, speeds[c], along_z, along_x, along_y)
            q = carry_back * q_ref[c, z] + step_size * slope
            out_ref[c, z - WIDE] = speeds[c] + second_gain * q
        return 0

    lax.fori_loop(WIDE, WIDE + depth, second_section, 0)

    pieces = sent_ref.shape[0]
    for s in range(pieces):
        place_ref[assign_ref[s]] = s
    pairs = across // 2
    for b in range(pieces):
        c, x = b // pairs, 2 * (b % pairs)
        to = place_ref[b]
        sent_ref[to, :, 0:lanes] = out_ref[c, :, x, :]
        sent_ref[to, :, lanes : 2 * lanes] = out_ref[c, :, x + 1, :]


def pair_index(i, j):
    return i * 4 - (i * (i - 1)) // 2 + (j - i)


def modes_gram_kernel(modes_ref, out_ref):
    count = modes_ref.shape[1] // BLOCK
    for i in range(count):
        for j in range(i, count):
            at = pair_index(i, j) * BLOCK
            out_ref[at : at + BLOCK, :] = product(
                modes_ref[:, i * BLOCK : (i + 1) * BLOCK], modes_ref[:, j * BLOCK : (j + 1) * BLOCK], ((0,), (0,))
            )


def snapshot_gram_kernel(planes_ref, received_ref, modes_ref, packed_in, packed_ref, snap_ref):
    count = snap_ref.shape[0]
    blocks = modes_ref.shape[1] // BLOCK
    base = pair_index(blocks - 1, blocks - 1) * BLOCK + BLOCK
    packed_ref[0:base, :] = packed_in[0:base, :]
    for k in range(count):
        snap_ref[k : k + 1, :] = received_ref[pl.ds(planes_ref[k], 1), :]
    snap = snap_ref[...]
    cross = product(modes_ref[...], snap, ((0,), (1,)))
    for b in range(blocks):
        at, side = base + (b // 2) * BLOCK, (b % 2) * count
        packed_ref[at : at + BLOCK, side : side + count] = cross[b * BLOCK : (b + 1) * BLOCK, :]
    packed_ref[BLOCK - count : BLOCK, 0:count] = product(snap, snap, ((1,), (1,)))


def lanes_of(value, j):
    return jnp.broadcast_to(value[:, j : j + 1], value.shape)


def row_of(value, i):
    return jnp.broadcast_to(value[i : i + 1, :], value.shape)


def total(terms):
    while len(terms) > 1:
        terms = [a + b for a, b in zip(terms[::2], terms[1::2])] + ([terms[-1]] if len(terms) % 2 else [])
    return terms[0]


def eliminate(main, side, upper_ref, inverse_ref, first, last, rows):
    sub = lax.broadcasted_iota(jnp.int32, (8, BLOCK), 0)
    lane = lax.broadcasted_iota(jnp.int32, (8, BLOCK), 1)
    for p in range(first, last):
        top, left = main[p], side[p]
        columns = [lanes_of(top, 8 * p + j) for j in range(8)]
        a = [[row_of(columns[j], i) if j <= i else None for j in range(8)] for i in range(8)]
        scale = [None] * 8
        for j in range(8):
            scale[j] = lax.rsqrt(a[j][j])
            for i in range(j + 1, 8):
                a[i][j] = a[i][j] * scale[j]
            for m in range(j + 1, 8):
                for i in range(m, 8):
                    a[i][m] = a[i][m] - a[i][j] * a[m][j]
        v = [[None] * 8 for _ in range(8)]
        for j in range(8):
            v[j][j] = scale[j]
            for i in range(j + 1, 8):
                v[i][j] = -scale[i] * total([a[i][k] * v[k][j] for k in range(j, i)])
        top_rows = [row_of(top, j) for j in range(8)]
        left_rows = [row_of(left, j) for j in range(8)]
        zero = jnp.zeros((8, BLOCK), jnp.float32)
        down, back = [], []
        for j in range(8):
            column, line = zero, zero
            for i in range(j, 8):
                column = jnp.where(sub == i, v[i][j], column)
            for i in range(j + 1):
                line = jnp.where(sub == i, v[j][i], line)
            down.append(column)
            back.append(line)
        upper = total([down[j] * top_rows[j] for j in range(8)])
        lower = total([down[j] * left_rows[j] for j in range(8)])
        upper_ref[8 * p : 8 * p + 8, :] = jnp.where(lane >= 8 * p + sub, upper, 0.0)
        inverse_ref[8 * p : 8 * p + 8, :] = lower
        if p + 1 == rows:
            break
        upper_rows = [row_of(upper, j) for j in range(8)]
        lower_rows = [row_of(lower, j) for j in range(8)]
        top = total([back[j] * upper_rows[j] for j in range(8)])
        left = total([back[j] * lower_rows[j] for j in range(8)])
        top_rows = [row_of(top, j) for j in range(8)]
        left_rows = [row_of(left, j) for j in range(8)]
        for i in range(p + 1, rows):
            here = [lanes_of(main[i], 8 * p + j) for j in range(8)]
            main[i] = main[i] - total([here[j] * top_rows[j] for j in range(8)])
            side[i] = side[i] - total([here[j] * left_rows[j] for j in range(8)])


def factor_kernel(packed_ref, modes_ref, snap_ref, basis_ref, factor_ref, block_ref, upper_ref, inverse_ref, work_ref, done_ref):
    count = snap_ref.shape[0]
    blocks = modes_ref.shape[1] // BLOCK
    half = BLOCK // 16
    base = pair_index(blocks - 1, blocks - 1) * BLOCK + BLOCK
    wide = blocks + 1
    lane = lax.broadcasted_iota(jnp.int32, (BLOCK, BLOCK), 1)
    sub = lax.broadcasted_iota(jnp.int32, (BLOCK, BLOCK), 0)
    unit = jnp.where(lane == sub, 1.0, 0.0)

    for i in range(blocks):
        for j in range(i, blocks):
            at = pair_index(i, j) * BLOCK
            value = packed_ref[at : at + BLOCK, :]
            if i == j:
                value = jnp.where(lane >= sub, value, value.T)
            block_ref[i * wide + j] = value
        at = base + (i // 2) * BLOCK
        pair = packed_ref[at : at + BLOCK, :]
        if i % 2:
            pair = pltpu.roll(pair, count, 1)
        block_ref[i * wide + blocks] = jnp.where(lane < count, pair, 0.0)
        work_ref[i] = modes_ref[:, i * BLOCK : (i + 1) * BLOCK]
    block_ref[blocks * wide + blocks] = unit
    block_ref[blocks * wide + blocks, 0:count, 0:count] = packed_ref[BLOCK - count : BLOCK, 0:count]
    work_ref[blocks] = jnp.zeros(work_ref.shape[1:], jnp.float32)
    work_ref[blocks, :, 0:count] = snap_ref[...].T

    def one_block(b, _):
        mine = b * wide + b
        rows = BLOCK // 8
        inverse_ref[...] = unit
        upper_ref[...] = unit
        main = [block_ref[mine, 8 * i : 8 * i + 8, :] for i in range(rows)]
        side = [inverse_ref[8 * i : 8 * i + 8, :] for i in range(rows)]
        eliminate(main, side, upper_ref, inverse_ref, 0, half, rows)

        @pl.when(b < blocks)
        def _():
            eliminate(main, side, upper_ref, inverse_ref, half, rows, rows)

        block_ref[mine] = upper_ref[...]
        inverse = inverse_ref[...]
        done = product(work_ref[b], inverse, ((1,), (1,)))
        done_ref[b] = done

        def along(j, _):
            block_ref[b * wide + j] = product(inverse, block_ref[b * wide + j], ((1,), (0,)))
            return 0

        lax.fori_loop(b + 1, wide, along, 0)

        def across(j, _):
            line = block_ref[b * wide + j]
            work_ref[j] = work_ref[j] - product(done, line, ((1,), (0,)))

            def down(i, _):
                block_ref[i * wide + j] = block_ref[i * wide + j] - product(block_ref[b * wide + i], line, ((0,), (0,)))
                return 0

            lax.fori_loop(b + 1, j + 1, down, 0)
            return 0

        lax.fori_loop(b + 1, wide, across, 0)
        return 0

    lax.fori_loop(0, wide, one_block, 0)

    for i in range(blocks):
        basis_ref[:, i * BLOCK : (i + 1) * BLOCK] = done_ref[i]
        for j in range(blocks):
            value = block_ref[i * wide + j] if j >= i else jnp.zeros((BLOCK, BLOCK), jnp.float32)
            factor_ref[i * BLOCK : (i + 1) * BLOCK, j * BLOCK : (j + 1) * BLOCK] = value
        factor_ref[i * BLOCK : (i + 1) * BLOCK, blocks * BLOCK :] = block_ref[i * wide + blocks, :, 0:count]
        factor_ref[blocks * BLOCK :, i * BLOCK : (i + 1) * BLOCK] = jnp.zeros((count, BLOCK), jnp.float32)
    basis_ref[:, blocks * BLOCK :] = done_ref[blocks, :, 0:count]
    factor_ref[blocks * BLOCK :, blocks * BLOCK :] = block_ref[blocks * wide + blocks, 0:count, 0:count]


def f32(*shape):
    return jax.ShapeDtypeStruct(shape, jnp.float32)


def sections(velocity, assign):
    comps, depth, across, height = velocity.shape
    before, after = both_ways(velocity[:, :, :WIDE], velocity[:, :, across - WIDE :], "grp", True)
    field = jnp.concatenate([velocity, after, before], axis=2)
    before, after = both_ways(field[:, :WIDE], field[:, depth - WIDE :], "slab", True)
    field = jnp.concatenate([before, field, after], axis=1)
    shape = field.shape
    tiles = -(-shape[0] * shape[1] * WIDE // height)
    packed = f32(tiles, shape[2], height)
    first, last = vmem_call(pack_kernel, [packed, packed], [VM], moved=4 * field.size)(field)
    before, after = both_ways(first, last, "row", False)
    where = jnp.stack([lax.axis_index("row"), lax.axis_size("row")]).astype(jnp.int32)
    pieces = comps * across // 2
    return vmem_call(
        sections_kernel,
        [f32(*velocity.shape), f32(pieces, depth, 2 * height)],
        [SM, SM, VM, VM, VM],
        scratch=[
            pltpu.VMEM((comps, shape[1], shape[2], 2 * height), jnp.float32),
            pltpu.VMEM((comps, shape[1], shape[2], 2 * height), jnp.float32),
            pltpu.VMEM((comps, shape[1], across, height), jnp.float32),
            pltpu.SMEM((pieces,), jnp.int32),
        ],
        moved=8 * velocity.size,
    )(assign, where, field, before, after)


def on_device(velocity, modes, planes, assign):
    count, rank, held = planes.shape[0], modes.shape[1], modes.shape[0]
    devices = lax.axis_size("grp") * lax.axis_size("slab") * lax.axis_size("row")
    blocks = rank // BLOCK
    rows = (blocks * (blocks + 1) // 2 + blocks // 2) * BLOCK
    packed = vmem_call(modes_gram_kernel, f32(rows, BLOCK), [VM], flops=12 * held * rank * rank, moved=4 * modes.size)(modes)

    advanced, sent = sections(velocity, assign)
    received = lax.all_to_all(sent, "slab", 0, 0, tiled=True).reshape(-1, sent.shape[2])
    packed, snap = vmem_call(
        snapshot_gram_kernel, [f32(rows, BLOCK), f32(count, held)], [SM, VM, VM, VM], aliases={3: 0}
    )(planes, received, modes, packed)

    shares = packed.reshape(devices, rows // devices, BLOCK)
    shares = lax.all_to_all(shares, ALL, 0, 0, tiled=True)
    share = jnp.sum(shares, axis=0, keepdims=True) * (1.0 / float(held * devices))
    gram = lax.all_to_all(jnp.broadcast_to(share, shares.shape), ALL, 0, 0, tiled=True)

    wide = blocks + 1
    basis, factor = vmem_call(
        factor_kernel,
        [f32(held, rank + count), f32(rank + count, rank + count)],
        [VM, VM, VM],
        scratch=[
            pltpu.VMEM((wide * wide, BLOCK, BLOCK), jnp.float32),
            pltpu.VMEM((BLOCK, BLOCK), jnp.float32),
            pltpu.VMEM((BLOCK, BLOCK), jnp.float32),
            pltpu.VMEM((wide, held, BLOCK), jnp.float32),
            pltpu.VMEM((wide, held, BLOCK), jnp.float32),
        ],
    )(gram.reshape(rows, BLOCK), modes, snap)
    return (advanced, basis, factor)


def solution(mesh):
    placed = (P(None, "slab", "grp", "row"), P(("grp", "slab", "row"), None), P(), P())
    return jax.shard_map(
        on_device,
        mesh=mesh,
        in_specs=placed,
        out_specs=(P(None, "slab", "grp", "row"), P(("grp", "slab", "row"), None), P()),
        check_vma=False,
    )
```

```python
import jax
import jax.numpy as jnp
from jax import lax
from jax.experimental import pallas as pl
from jax.experimental.pallas import tpu as pltpu
from jax.sharding import PartitionSpec as P

step_size = 0.05
viscosity = 1.0
third = 1.0 / 3.0
carry_back = -5.0 / 9.0
second_gain = 15.0 / 16.0

ALL = ("grp", "slab", "row")
WIDE = 4
BLOCK = 128
VMEM_LIMIT = 48 * 1024 * 1024


def vmem_call(kernel, out_shape, in_specs, scratch=(), aliases=None, flops=0, moved=0):
    single = not isinstance(out_shape, (list, tuple))
    whole = pl.BlockSpec(memory_space=pltpu.VMEM)
    return pl.pallas_call(
        kernel,
        out_shape=out_shape,
        in_specs=in_specs,
        out_specs=whole if single else [whole] * len(out_shape),
        scratch_shapes=list(scratch),
        input_output_aliases=aliases or {},
        cost_estimate=pl.CostEstimate(flops=flops, bytes_accessed=moved, transcendentals=0),
        compiler_params=pltpu.CompilerParams(vmem_limit_bytes=VMEM_LIMIT),
    )


VM = pl.BlockSpec(memory_space=pltpu.VMEM)
SM = pl.BlockSpec(memory_space=pltpu.SMEM)


def product(left, right, dims):
    return lax.dot_general(
        left,
        right,
        (dims, ((), ())),
        precision=lax.Precision.HIGHEST,
        preferred_element_type=jnp.float32,
    )


def both_ways(low, high, axis, wrap):
    devices = lax.axis_size(axis)
    up = [(i, (i + 1) % devices) for i in range(devices if wrap else devices - 1)]
    down = [(j, i) for i, j in up]
    return lax.ppermute(high, axis, up), lax.ppermute(low, axis, down)


def pack_kernel(field_ref, first_ref, last_ref):
    comps, depth, rows, lanes = field_ref.shape
    planes = comps * depth
    group = lanes // WIDE
    lane = lax.broadcasted_iota(jnp.int32, (rows, lanes), 1)
    for tile in range(first_ref.shape[0]):
        head = jnp.zeros((rows, lanes), jnp.float32)
        tail = jnp.zeros((rows, lanes), jnp.float32)
        for q in range(min(group, planes - tile * group)):
            c, z = divmod(tile * group + q, depth)
            value = field_ref[c, z]
            here = (lane >= WIDE * q) & (lane < WIDE * (q + 1))
            head = jnp.where(here, pltpu.roll(value, (WIDE * q) % lanes, 1), head)
            tail = jnp.where(here, pltpu.roll(value, (WIDE * (q + 1)) % lanes, 1), tail)
        first_ref[tile] = head
        last_ref[tile] = tail


def parts_of(value, axis):
    size = value.shape[axis]
    return [pltpu.roll(value, shift % size, axis) for shift in (2, 1, -1, -2)]


def derivatives(parts, centre):
    far = parts[0], parts[3]
    first = ((far[0] - far[1]) + 8.0 * (parts[2] - parts[1])) * (1.0 / 12.0)
    second = (16.0 * (parts[1] + parts[2]) - (far[0] + far[1]) - 30.0 * centre) * (1.0 / 12.0)
    return first, second


def sections_kernel(
    assign_ref, row_ref, field_ref, before_ref, after_ref, out_ref, sent_ref, wide_ref, mid_ref, q_ref, place_ref
):
    comps, depth_wide, rows, lanes = field_ref.shape
    depth, across = out_ref.shape[1], out_ref.shape[2]
    group = lanes // WIDE
    lane = lax.broadcasted_iota(jnp.int32, (rows, lanes), 1)

    for c in range(comps):
        for z in range(depth_wide):
            tile, q = divmod(c * depth_wide + z, group)
            after = pltpu.roll(after_ref[tile], (-WIDE * q) % lanes, 1)
            before = pltpu.roll(before_ref[tile], (-WIDE * (q + 1)) % lanes, 1)
            halo = jnp.where(lane < WIDE, after, jnp.where(lane >= lanes - WIDE, before, 0.0))
            wide_ref[c, z, :, 0:lanes] = field_ref[c, z]
            wide_ref[c, z, :, lanes : 2 * lanes] = halo

    edge = lax.broadcasted_iota(jnp.int32, (rows, 2 * lanes), 1)
    outside = ((edge >= lanes + lanes // 2) & (row_ref[0] == 0)) | (
        (edge >= lanes) & (edge < lanes + lanes // 2) & (row_ref[0] == row_ref[1] - 1)
    )

    def tendency(speeds, centre, along_z, along_x, along_y):
        dz_first, dz_second = derivatives(along_z, centre)
        dx_first, dx_second = derivatives(along_x, centre)
        dy_first, dy_second = derivatives(along_y, centre)
        convect = speeds[0] * dx_first + speeds[1] * dy_first + speeds[2] * dz_first
        return viscosity * (dx_second + dy_second + dz_second) - convect

    def first_section(z, _):
        speeds = [wide_ref[c, z] for c in range(comps)]
        for c in range(comps):
            along_z = [wide_ref[c, z + k] for k in (-2, -1, 1, 2)]
            slope = tendency(speeds, speeds[c], along_z, parts_of(speeds[c], 0), parts_of(speeds[c], 1))
            q = step_size * slope
            mid_ref[c, z] = jnp.where(outside, 0.0, speeds[c] + third * q)
            q_ref[c, z] = q[:across, :lanes]
        return 0

    lax.fori_loop(2, depth_wide - 2, first_section, 0)

    def second_section(z, _):
        speeds = [mid_ref[c, z, 0:across, 0:lanes] for c in range(comps)]
        for c in range(comps):
            along_z = [mid_ref[c, z + k, 0:across, 0:lanes] for k in (-2, -1, 1, 2)]
            along_x = [p[:across] for p in parts_of(mid_ref[c, z, :, 0:lanes], 0)]
            along_y = [p[:, :lanes] for p in parts_of(mid_ref[c, z, 0:across, :], 1)]
            slope = tendency(speeds, speeds[c], along_z, along_x, along_y)
            q = carry_back * q_ref[c, z] + step_size * slope
            out_ref[c, z - WIDE] = speeds[c] + second_gain * q
        return 0

    lax.fori_loop(WIDE, WIDE + depth, second_section, 0)

    pieces = sent_ref.shape[0]
    for s in range(pieces):
        place_ref[assign_ref[s]] = s
    pairs = across // 2
    for b in range(pieces):
        c, x = b // pairs, 2 * (b % pairs)
        to = place_ref[b]
        sent_ref[to, :, 0:lanes] = out_ref[c, :, x, :]
        sent_ref[to, :, lanes : 2 * lanes] = out_ref[c, :, x + 1, :]


def pair_index(i, j):
    return i * 4 - (i * (i - 1)) // 2 + (j - i)


def modes_gram_kernel(modes_ref, out_ref):
    count = modes_ref.shape[1] // BLOCK
    for i in range(count):
        for j in range(i, count):
            at = pair_index(i, j) * BLOCK
            out_ref[at : at + BLOCK, :] = product(
                modes_ref[:, i * BLOCK : (i + 1) * BLOCK], modes_ref[:, j * BLOCK : (j + 1) * BLOCK], ((0,), (0,))
            )


def snapshot_gram_kernel(planes_ref, received_ref, modes_ref, packed_ref, snap_ref):
    count = snap_ref.shape[0]
    blocks = modes_ref.shape[1] // BLOCK
    for k in range(count):
        snap_ref[k : k + 1, :] = received_ref[pl.ds(planes_ref[k], 1), :]
    snap = snap_ref[...]
    cross = product(modes_ref[...], snap, ((0,), (1,)))
    for b in range(blocks):
        at, side = (b // 2) * BLOCK, (b % 2) * count
        packed_ref[at : at + BLOCK, side : side + count] = cross[b * BLOCK : (b + 1) * BLOCK, :]
    base = blocks // 2 * BLOCK
    packed_ref[base : base + count, :] = jnp.zeros((count, BLOCK), jnp.float32)
    packed_ref[base : base + count, 0:count] = product(snap, snap, ((1,), (1,)))


def lanes_of(value, j):
    return jnp.broadcast_to(value[:, j : j + 1], value.shape)


def row_of(value, i):
    return jnp.broadcast_to(value[i : i + 1, :], value.shape)


def total(terms):
    while len(terms) > 1:
        terms = [a + b for a, b in zip(terms[::2], terms[1::2])] + ([terms[-1]] if len(terms) % 2 else [])
    return terms[0]


def eliminate(main, side, upper_ref, inverse_ref, first, last, rows):
    sub = lax.broadcasted_iota(jnp.int32, (8, BLOCK), 0)
    lane = lax.broadcasted_iota(jnp.int32, (8, BLOCK), 1)
    for p in range(first, last):
        top, left = main[p], side[p]
        columns = [lanes_of(top, 8 * p + j) for j in range(8)]
        a = [[row_of(columns[j], i) if j <= i else None for j in range(8)] for i in range(8)]
        scale = [None] * 8
        for j in range(8):
            scale[j] = lax.rsqrt(a[j][j])
            for i in range(j + 1, 8):
                a[i][j] = a[i][j] * scale[j]
            for m in range(j + 1, 8):
                for i in range(m, 8):
                    a[i][m] = a[i][m] - a[i][j] * a[m][j]
        v = [[None] * 8 for _ in range(8)]
        for j in range(8):
            v[j][j] = scale[j]
            for i in range(j + 1, 8):
                v[i][j] = -scale[i] * total([a[i][k] * v[k][j] for k in range(j, i)])
        top_rows = [row_of(top, j) for j in range(8)]
        left_rows = [row_of(left, j) for j in range(8)]
        zero = jnp.zeros((8, BLOCK), jnp.float32)
        down, back = [], []
        for j in range(8):
            column, line = zero, zero
            for i in range(j, 8):
                column = jnp.where(sub == i, v[i][j], column)
            for i in range(j + 1):
                line = jnp.where(sub == i, v[j][i], line)
            down.append(column)
            back.append(line)
        upper = total([down[j] * top_rows[j] for j in range(8)])
        lower = total([down[j] * left_rows[j] for j in range(8)])
        upper_ref[8 * p : 8 * p + 8, :] = jnp.where(lane >= 8 * p + sub, upper, 0.0)
        inverse_ref[8 * p : 8 * p + 8, :] = lower
        if p + 1 == rows:
            break
        upper_rows = [row_of(upper, j) for j in range(8)]
        lower_rows = [row_of(lower, j) for j in range(8)]
        top = total([back[j] * upper_rows[j] for j in range(8)])
        left = total([back[j] * lower_rows[j] for j in range(8)])
        top_rows = [row_of(top, j) for j in range(8)]
        left_rows = [row_of(left, j) for j in range(8)]
        for i in range(p + 1, rows):
            here = [lanes_of(main[i], 8 * p + j) for j in range(8)]
            main[i] = main[i] - total([here[j] * top_rows[j] for j in range(8)])
            side[i] = side[i] - total([here[j] * left_rows[j] for j in range(8)])


def identity(size):
    lane = lax.broadcasted_iota(jnp.int32, (size, size), 1)
    sub = lax.broadcasted_iota(jnp.int32, (size, size), 0)
    return jnp.where(lane == sub, 1.0, 0.0)


def pair_rows(i, j):
    at = pair_index(i, j) * BLOCK
    return slice(at, at + BLOCK)


def factor_step(b, blocks, gram_ref, side_in, block_ref, side_ref, upper_ref, inverse_ref):
    rows = BLOCK // 8
    lane = lax.broadcasted_iota(jnp.int32, (BLOCK, BLOCK), 1)
    sub = lax.broadcasted_iota(jnp.int32, (BLOCK, BLOCK), 0)
    value = gram_ref[pair_rows(b, b), :]
    value = jnp.where(lane >= sub, value, value.T)
    unit = identity(BLOCK)
    main = [value[8 * i : 8 * i + 8, :] for i in range(rows)]
    side = [unit[8 * i : 8 * i + 8, :] for i in range(rows)]
    eliminate(main, side, upper_ref, inverse_ref, 0, rows, rows)
    inverse = inverse_ref[...]
    for i in range(b):
        for j in range(i, blocks):
            block_ref[pair_rows(i, j), :] = gram_ref[pair_rows(i, j), :]
            if j < b:
                side_ref[pair_rows(i, j), :] = side_in[pair_rows(i, j), :]
    block_ref[pair_rows(b, b), :] = upper_ref[...]
    side_ref[pair_rows(b, b), :] = inverse
    for j in range(b):
        side_ref[pair_rows(j, b), :] = product(inverse, side_in[pair_rows(j, b), :], ((1,), (0,)))
    for j in range(b + 1, blocks):
        block_ref[pair_rows(b, j), :] = product(inverse, gram_ref[pair_rows(b, j), :], ((1,), (0,)))
    for i in range(b + 1, blocks):
        factor = block_ref[pair_rows(b, i), :]
        for j in range(i, blocks):
            taken = product(factor, block_ref[pair_rows(b, j), :], ((0,), (0,)))
            block_ref[pair_rows(i, j), :] = gram_ref[pair_rows(i, j), :] - taken
        for j in range(b):
            taken = product(factor, side_ref[pair_rows(j, b), :], ((0,), (0,)))
            side_ref[pair_rows(j, i), :] = side_in[pair_rows(j, i), :] - taken
        side_ref[pair_rows(b, i), :] = -product(factor, inverse, ((0,), (0,)))


def first_factor_kernel(gram_ref, block_ref, side_ref, upper_ref, inverse_ref):
    factor_step(0, 4, gram_ref, None, block_ref, side_ref, upper_ref, inverse_ref)


def next_factor_kernel(b):
    def next_factor(gram_ref, side_in, block_ref, side_ref, upper_ref, inverse_ref):
        factor_step(b, 4, gram_ref, side_in, block_ref, side_ref, upper_ref, inverse_ref)

    return next_factor


def last_factor_kernel(gram_ref, side_in, modes_ref, upper_out, inverse_out, done_ref, block_ref, side_ref, upper_ref, inverse_ref):
    blocks = modes_ref.shape[1] // BLOCK
    factor_step(blocks - 1, blocks, gram_ref, side_in, block_ref, side_ref, upper_ref, inverse_ref)
    zero = jnp.zeros((BLOCK, BLOCK), jnp.float32)
    for i in range(blocks):
        for j in range(blocks):
            here = (slice(i * BLOCK, (i + 1) * BLOCK), slice(j * BLOCK, (j + 1) * BLOCK))
            upper_out[here] = block_ref[pair_rows(i, j), :] if i <= j else zero
            inverse_out[here] = side_ref[pair_rows(j, i), :] if j <= i else zero
    for i in range(blocks):
        size = (i + 1) * BLOCK
        done_ref[i * BLOCK : size, :] = product(inverse_out[i * BLOCK : size, 0:size], modes_ref[:, 0:size], ((1,), (1,)))


def finish_kernel(packed_ref, snap_ref, upper_ref, inverse_ref, done_ref, basis_ref, factor_ref, cross_ref, corner_ref, back_ref):
    count = snap_ref.shape[0]
    rank = upper_ref.shape[0]
    blocks = rank // BLOCK
    base = blocks // 2 * BLOCK
    for i in range(blocks):
        at, side = (i // 2) * BLOCK, (i % 2) * count
        cross_ref[i * BLOCK : (i + 1) * BLOCK, :] = packed_ref[at : at + BLOCK, side : side + count]
    cross = product(inverse_ref[...], cross_ref[...], ((1,), (0,)))
    rows = count // 8
    corner_ref[...] = jnp.zeros_like(corner_ref)
    corner_ref[:, 0:count] = packed_ref[base : base + count, 0:count] - product(cross, cross, ((0,), (0,)))
    unit = identity(BLOCK)
    main = [corner_ref[8 * i : 8 * i + 8, :] for i in range(rows)]
    side = [unit[8 * i : 8 * i + 8, :] for i in range(rows)]
    eliminate(main, side, corner_ref, back_ref, 0, rows, rows)
    rest = snap_ref[...] - product(cross, done_ref[...], ((0,), (0,)))
    basis_ref[0:rank, :] = done_ref[...]
    basis_ref[rank:, :] = product(back_ref[:, 0:count], rest, ((1,), (0,)))
    factor_ref[0:rank, 0:rank] = upper_ref[...]
    factor_ref[0:rank, rank:] = cross
    factor_ref[rank:, 0:rank] = jnp.zeros((count, rank), jnp.float32)
    factor_ref[rank:, rank:] = corner_ref[:, 0:count]


def f32(*shape):
    return jax.ShapeDtypeStruct(shape, jnp.float32)


def together(*values):
    return lax.optimization_barrier(values)


def halo_field(velocity, first, last, packed):
    depth = velocity.shape[1]
    before, after = both_ways(first, last, "grp", True)
    share = scattered_sum(packed, "grp")
    before, after, share = together(before, after, share)
    field = jnp.concatenate([velocity, after, before], axis=2)
    before, after = both_ways(field[:, :WIDE], field[:, depth - WIDE :], "slab", True)
    share = scattered_sum(share, "row")
    before, after, share = together(before, after, share)
    field = jnp.concatenate([before, field, after], axis=1)
    shape = field.shape
    tiles = -(-shape[0] * shape[1] * WIDE // shape[3])
    edge = f32(tiles, shape[2], shape[3])
    first, last = vmem_call(pack_kernel, [edge, edge], [VM], moved=4 * field.size)(field)
    before, after = both_ways(first, last, "row", False)
    share = jnp.sum(everyones(share, "slab"), axis=0)
    return (field,) + tuple(together(before, after, share))


def sections(field, before, after, assign, depth, across):
    comps, height = field.shape[0], field.shape[3]
    where = jnp.stack([lax.axis_index("row"), lax.axis_size("row")]).astype(jnp.int32)
    pieces = comps * across // 2
    wide = (comps, field.shape[1], field.shape[2], 2 * height)
    return vmem_call(
        sections_kernel,
        [f32(comps, depth, across, height), f32(pieces, depth, 2 * height)],
        [SM, SM, VM, VM, VM],
        scratch=[
            pltpu.VMEM(wide, jnp.float32),
            pltpu.VMEM(wide, jnp.float32),
            pltpu.VMEM((comps, field.shape[1], across, height), jnp.float32),
            pltpu.SMEM((pieces,), jnp.int32),
        ],
        moved=32 * field.size,
    )(assign, where, field, before, after)


def scattered_sum(value, axis):
    shares = value.reshape(lax.axis_size(axis), -1, value.shape[1])
    return jnp.sum(lax.all_to_all(shares, axis, 0, 0, tiled=True), axis=0)


def everyones(value, axis):
    copies = jnp.broadcast_to(value[None], (lax.axis_size(axis),) + value.shape)
    return lax.all_to_all(copies, axis, 0, 0, tiled=True)


def on_device(velocity, modes, planes, assign):
    count, rank, held = planes.shape[0], modes.shape[1], modes.shape[0]
    devices = lax.axis_size("grp") * lax.axis_size("slab") * lax.axis_size("row")
    scale = 1.0 / float(held * devices)
    blocks = rank // BLOCK
    rows = blocks * (blocks + 1) // 2 * BLOCK
    tall = blocks // 2 * BLOCK + count
    block = [pltpu.VMEM((BLOCK, BLOCK), jnp.float32)] * 2
    state = [f32(rows, BLOCK), f32(rows, BLOCK)]
    cost = 7 * 1000 * 1000 * 1000

    across = velocity.shape[2]
    first, last = velocity[:, :, :WIDE], velocity[:, :, across - WIDE :]
    packed = vmem_call(modes_gram_kernel, f32(rows, BLOCK), [VM], flops=12 * held * rank * rank, moved=4 * modes.size)(modes)
    field, before, after, share = halo_field(velocity, first, last, packed)
    share = everyones(share * scale, "row").reshape(-1, BLOCK)
    advanced, sent = sections(field, before, after, assign, velocity.shape[1], velocity.shape[2])
    sent, share = together(sent, share)
    received = lax.all_to_all(sent, "slab", 0, 0, tiled=True).reshape(-1, sent.shape[2])
    packed, snap = vmem_call(snapshot_gram_kernel, [f32(tall, BLOCK), f32(count, held)], [SM, VM, VM])(planes, received, modes)

    groups = lax.axis_size("grp")
    part = tall // groups
    copies = jnp.broadcast_to(share[None], (groups,) + share.shape)
    both = jnp.concatenate([packed.reshape(groups, part, BLOCK), copies], axis=1)
    both = lax.all_to_all(both, "grp", 0, 0, tiled=True)
    share = jnp.sum(both[:, :part], axis=0)
    gram = both[:, part:].reshape(rows, BLOCK)

    lower = vmem_call(first_factor_kernel, state, [VM], scratch=block, flops=cost)(gram)
    lower = vmem_call(next_factor_kernel(1), state, [VM, VM], scratch=block, flops=cost)(*lower)
    share = jnp.sum(everyones(share, "row"), axis=0)
    share, *lower = together(share, *lower)
    lower = vmem_call(next_factor_kernel(2), state, [VM, VM], scratch=block, flops=cost)(*lower)
    share = jnp.sum(everyones(share, "slab"), axis=0) * scale
    share, *lower = together(share, *lower)
    packed = everyones(share, "grp").reshape(tall, BLOCK)
    upper, inverse, done = vmem_call(
        last_factor_kernel,
        [f32(rank, rank), f32(rank, rank), f32(rank, held)],
        [VM, VM, VM],
        scratch=[pltpu.VMEM((rows, BLOCK), jnp.float32)] * 2 + block,
        flops=cost,
    )(*lower, modes)
    basis, factor = vmem_call(
        finish_kernel,
        [f32(rank + count, held), f32(rank + count, rank + count)],
        [VM, VM, VM, VM, VM],
        scratch=[
            pltpu.VMEM((rank, count), jnp.float32),
            pltpu.VMEM((count, BLOCK), jnp.float32),
            pltpu.VMEM((count, BLOCK), jnp.float32),
        ],
    )(packed, snap, upper, inverse, done)
    return (advanced, basis.T, factor)


def solution(mesh):
    placed = (P(None, "slab", "grp", "row"), P(("grp", "slab", "row"), None), P(), P())
    return jax.shard_map(
        on_device,
        mesh=mesh,
        in_specs=placed,
        out_specs=(P(None, "slab", "grp", "row"), P(("grp", "slab", "row"), None), P()),
        check_vma=False,
    )
```

```python
import jax
import jax.numpy as jnp
from jax import lax
from jax.experimental import pallas as pl
from jax.experimental.pallas import tpu as pltpu
from jax.sharding import PartitionSpec as P

step_size = 0.05
viscosity = 1.0
third = 1.0 / 3.0
carry_back = -5.0 / 9.0
second_gain = 15.0 / 16.0

ALL = ("grp", "slab", "row")
WIDE = 4
BLOCK = 128
VMEM_LIMIT = 48 * 1024 * 1024


def vmem_call(kernel, out_shape, in_specs, scratch=(), aliases=None, flops=0, moved=0):
    single = not isinstance(out_shape, (list, tuple))
    whole = pl.BlockSpec(memory_space=pltpu.VMEM)
    return pl.pallas_call(
        kernel,
        out_shape=out_shape,
        in_specs=in_specs,
        out_specs=whole if single else [whole] * len(out_shape),
        scratch_shapes=list(scratch),
        input_output_aliases=aliases or {},
        cost_estimate=pl.CostEstimate(flops=flops, bytes_accessed=moved, transcendentals=0),
        compiler_params=pltpu.CompilerParams(vmem_limit_bytes=VMEM_LIMIT),
    )


VM = pl.BlockSpec(memory_space=pltpu.VMEM)
SM = pl.BlockSpec(memory_space=pltpu.SMEM)


def product(left, right, dims):
    return lax.dot_general(
        left,
        right,
        (dims, ((), ())),
        precision=lax.Precision.HIGHEST,
        preferred_element_type=jnp.float32,
    )


def both_ways(low, high, axis, wrap):
    devices = lax.axis_size(axis)
    up = [(i, (i + 1) % devices) for i in range(devices if wrap else devices - 1)]
    down = [(j, i) for i, j in up]
    return lax.ppermute(high, axis, up), lax.ppermute(low, axis, down)


def pack_kernel(row_ref, field_ref, out_ref):
    comps, depth, rows, lanes = field_ref.shape
    planes = comps * depth
    group = lanes // WIDE
    lane = lax.broadcasted_iota(jnp.int32, (rows, lanes), 1)
    row, last = row_ref[0], row_ref[1] - 1
    heads, tails = [], []
    for tile in range(out_ref.shape[1]):
        head = jnp.zeros((rows, lanes), jnp.float32)
        tail = jnp.zeros((rows, lanes), jnp.float32)
        for q in range(min(group, planes - tile * group)):
            c, z = divmod(tile * group + q, depth)
            value = field_ref[c, z]
            here = (lane >= WIDE * q) & (lane < WIDE * (q + 1))
            head = jnp.where(here, pltpu.roll(value, (WIDE * q) % lanes, 1), head)
            tail = jnp.where(here, pltpu.roll(value, (WIDE * (q + 1)) % lanes, 1), tail)
        heads.append(head)
        tails.append(tail)

    @pl.when(row > 0)
    def _():
        for tile, head in enumerate(heads):
            out_ref[jnp.maximum(row - 1, 0), tile] = head

    @pl.when(row < last)
    def _():
        for tile, tail in enumerate(tails):
            out_ref[jnp.minimum(row + 1, last), tile] = tail


def parts_of(value, axis):
    size = value.shape[axis]
    return [pltpu.roll(value, shift % size, axis) for shift in (2, 1, -1, -2)]


def derivatives(parts, centre):
    far = parts[0], parts[3]
    first = ((far[0] - far[1]) + 8.0 * (parts[2] - parts[1])) * (1.0 / 12.0)
    second = (16.0 * (parts[1] + parts[2]) - (far[0] + far[1]) - 30.0 * centre) * (1.0 / 12.0)
    return first, second


def sections_kernel(
    assign_ref, row_ref, field_ref, edges_ref, out_ref, sent_ref, wide_ref, mid_ref, q_ref, place_ref
):
    comps, depth_wide, rows, lanes = field_ref.shape
    depth, across = out_ref.shape[1], out_ref.shape[2]
    group = lanes // WIDE
    lane = lax.broadcasted_iota(jnp.int32, (rows, lanes), 1)

    row, last = row_ref[0], row_ref[1] - 1
    previous, following = jnp.maximum(row - 1, 0), jnp.minimum(row + 1, last)
    from_next = (lane < WIDE) & (row < last)
    from_previous = (lane >= lanes - WIDE) & (row > 0)

    for c in range(comps):
        for z in range(depth_wide):
            tile, q = divmod(c * depth_wide + z, group)
            after = pltpu.roll(edges_ref[following, tile], (-WIDE * q) % lanes, 1)
            before = pltpu.roll(edges_ref[previous, tile], (-WIDE * (q + 1)) % lanes, 1)
            halo = jnp.where(from_next, after, jnp.where(from_previous, before, 0.0))
            wide_ref[c, z, :, 0:lanes] = field_ref[c, z]
            wide_ref[c, z, :, lanes : 2 * lanes] = halo

    edge = lax.broadcasted_iota(jnp.int32, (rows, 2 * lanes), 1)
    outside = ((edge >= lanes + lanes // 2) & (row == 0)) | ((edge >= lanes) & (edge < lanes + lanes // 2) & (row == last))

    def tendency(speeds, centre, along_z, along_x, along_y):
        dz_first, dz_second = derivatives(along_z, centre)
        dx_first, dx_second = derivatives(along_x, centre)
        dy_first, dy_second = derivatives(along_y, centre)
        convect = speeds[0] * dx_first + speeds[1] * dy_first + speeds[2] * dz_first
        return viscosity * (dx_second + dy_second + dz_second) - convect

    def first_section(z, _):
        speeds = [wide_ref[c, z] for c in range(comps)]
        for c in range(comps):
            along_z = [wide_ref[c, z + k] for k in (-2, -1, 1, 2)]
            slope = tendency(speeds, speeds[c], along_z, parts_of(speeds[c], 0), parts_of(speeds[c], 1))
            q = step_size * slope
            mid_ref[c, z] = jnp.where(outside, 0.0, speeds[c] + third * q)
            q_ref[c, z] = q[:across, :lanes]
        return 0

    lax.fori_loop(2, depth_wide - 2, first_section, 0)

    def second_section(z, _):
        speeds = [mid_ref[c, z, 0:across, 0:lanes] for c in range(comps)]
        for c in range(comps):
            along_z = [mid_ref[c, z + k, 0:across, 0:lanes] for k in (-2, -1, 1, 2)]
            along_x = [p[:across] for p in parts_of(mid_ref[c, z, :, 0:lanes], 0)]
            along_y = [p[:, :lanes] for p in parts_of(mid_ref[c, z, 0:across, :], 1)]
            slope = tendency(speeds, speeds[c], along_z, along_x, along_y)
            q = carry_back * q_ref[c, z] + step_size * slope
            out_ref[c, z - WIDE] = speeds[c] + second_gain * q
        return 0

    lax.fori_loop(WIDE, WIDE + depth, second_section, 0)

    pieces = sent_ref.shape[0]
    for s in range(pieces):
        place_ref[assign_ref[s]] = s
    pairs = across // 2
    for b in range(pieces):
        c, x = b // pairs, 2 * (b % pairs)
        to = place_ref[b]
        sent_ref[to, 0:depth, :] = out_ref[c, :, x, :]
        sent_ref[to, depth : 2 * depth, :] = out_ref[c, :, x + 1, :]


def pair_index(i, j):
    return i * 4 - (i * (i - 1)) // 2 + (j - i)


def modes_gram_kernel(modes_ref, out_ref):
    count = modes_ref.shape[1] // BLOCK
    for i in range(count):
        for j in range(i, count):
            at = pair_index(i, j) * BLOCK
            out_ref[at : at + BLOCK, :] = product(
                modes_ref[:, i * BLOCK : (i + 1) * BLOCK], modes_ref[:, j * BLOCK : (j + 1) * BLOCK], ((0,), (0,))
            )


def snapshot_gram_kernel(planes_ref, received_ref, modes_ref, out_ref, snap_ref, packed_ref):
    count, held = snap_ref.shape
    slabs = received_ref.shape[0]
    blocks = modes_ref.shape[1] // BLOCK
    tall = packed_ref.shape[0]
    groups, share = out_ref.shape[0], tall // out_ref.shape[0]
    ours = out_ref.shape[1] - share
    depth = (received_ref.shape[1] - ours) // 2
    for k in range(count):
        slab, z = planes_ref[k] // depth, planes_ref[k] % depth
        snap_ref[k : k + 1, 0:BLOCK] = received_ref[slab, pl.ds(z, 1), :]
        snap_ref[k : k + 1, BLOCK:held] = received_ref[slab, pl.ds(z + depth, 1), :]
    snap = snap_ref[...]
    cross = product(modes_ref[...], snap, ((0,), (1,)))
    for b in range(blocks):
        at, side = (b // 2) * BLOCK, (b % 2) * count
        packed_ref[at : at + BLOCK, side : side + count] = cross[b * BLOCK : (b + 1) * BLOCK, :]
    base = blocks // 2 * BLOCK
    packed_ref[base : base + count, :] = jnp.zeros((count, BLOCK), jnp.float32)
    packed_ref[base : base + count, 0:count] = product(snap, snap, ((1,), (1,)))
    summed = total([received_ref[s, 2 * depth :, :] for s in range(slabs)])
    for g in range(groups):
        out_ref[g, 0:share, :] = packed_ref[g * share : (g + 1) * share, :]
        out_ref[g, share:, :] = summed


def lanes_of(value, j):
    return jnp.broadcast_to(value[:, j : j + 1], value.shape)


def row_of(value, i):
    return jnp.broadcast_to(value[i : i + 1, :], value.shape)


def total(terms):
    while len(terms) > 1:
        terms = [a + b for a, b in zip(terms[::2], terms[1::2])] + ([terms[-1]] if len(terms) % 2 else [])
    return terms[0]


def eliminate(main, side, upper_ref, inverse_ref, first, last, rows):
    sub = lax.broadcasted_iota(jnp.int32, (8, BLOCK), 0)
    lane = lax.broadcasted_iota(jnp.int32, (8, BLOCK), 1)
    for p in range(first, last):
        top, left = main[p], side[p]
        columns = [lanes_of(top, 8 * p + j) for j in range(8)]
        a = [[row_of(columns[j], i) if j <= i else None for j in range(8)] for i in range(8)]
        scale = [None] * 8
        for j in range(8):
            scale[j] = lax.rsqrt(a[j][j])
            for i in range(j + 1, 8):
                a[i][j] = a[i][j] * scale[j]
            for m in range(j + 1, 8):
                for i in range(m, 8):
                    a[i][m] = a[i][m] - a[i][j] * a[m][j]
        v = [[None] * 8 for _ in range(8)]
        for j in range(8):
            v[j][j] = scale[j]
            for i in range(j + 1, 8):
                v[i][j] = -scale[i] * total([a[i][k] * v[k][j] for k in range(j, i)])
        top_rows = [row_of(top, j) for j in range(8)]
        left_rows = [row_of(left, j) for j in range(8)]
        zero = jnp.zeros((8, BLOCK), jnp.float32)
        down, back = [], []
        for j in range(8):
            column, line = zero, zero
            for i in range(j, 8):
                column = jnp.where(sub == i, v[i][j], column)
            for i in range(j + 1):
                line = jnp.where(sub == i, v[j][i], line)
            down.append(column)
            back.append(line)
        upper = total([down[j] * top_rows[j] for j in range(8)])
        lower = total([down[j] * left_rows[j] for j in range(8)])
        upper_ref[8 * p : 8 * p + 8, :] = jnp.where(lane >= 8 * p + sub, upper, 0.0)
        inverse_ref[8 * p : 8 * p + 8, :] = lower
        if p + 1 == rows:
            break
        upper_rows = [row_of(upper, j) for j in range(8)]
        lower_rows = [row_of(lower, j) for j in range(8)]
        top = total([back[j] * upper_rows[j] for j in range(8)])
        left = total([back[j] * lower_rows[j] for j in range(8)])
        top_rows = [row_of(top, j) for j in range(8)]
        left_rows = [row_of(left, j) for j in range(8)]
        for i in range(p + 1, rows):
            here = [lanes_of(main[i], 8 * p + j) for j in range(8)]
            main[i] = main[i] - total([here[j] * top_rows[j] for j in range(8)])
            side[i] = side[i] - total([here[j] * left_rows[j] for j in range(8)])


def identity(size):
    lane = lax.broadcasted_iota(jnp.int32, (size, size), 1)
    sub = lax.broadcasted_iota(jnp.int32, (size, size), 0)
    return jnp.where(lane == sub, 1.0, 0.0)


def pair_rows(i, j):
    at = pair_index(i, j) * BLOCK
    return slice(at, at + BLOCK)


def modes_factor_kernel(gathered_ref, modes_ref, upper_out, inverse_out, done_ref, block_ref, side_ref, upper_ref, inverse_ref):
    blocks = modes_ref.shape[1] // BLOCK
    groups = gathered_ref.shape[0]
    each = block_ref.shape[0] // groups
    rows = BLOCK // 8
    lane = lax.broadcasted_iota(jnp.int32, (BLOCK, BLOCK), 1)
    sub = lax.broadcasted_iota(jnp.int32, (BLOCK, BLOCK), 0)
    unit = identity(BLOCK)
    zero = jnp.zeros((BLOCK, BLOCK), jnp.float32)
    for g in range(groups):
        block_ref[g * each : (g + 1) * each, :] = gathered_ref[g, gathered_ref.shape[1] - each :, :]
    for b in range(blocks):
        value = block_ref[pair_rows(b, b), :]
        value = jnp.where(lane >= sub, value, value.T)
        main = [value[8 * i : 8 * i + 8, :] for i in range(rows)]
        side = [unit[8 * i : 8 * i + 8, :] for i in range(rows)]
        eliminate(main, side, upper_ref, inverse_ref, 0, rows, rows)
        inverse = inverse_ref[...]
        block_ref[pair_rows(b, b), :] = upper_ref[...]
        side_ref[pair_rows(b, b), :] = inverse
        for j in range(b):
            side_ref[pair_rows(j, b), :] = product(inverse, side_ref[pair_rows(j, b), :], ((1,), (0,)))
        for j in range(b + 1, blocks):
            block_ref[pair_rows(b, j), :] = product(inverse, block_ref[pair_rows(b, j), :], ((1,), (0,)))
        for i in range(b + 1, blocks):
            factor = block_ref[pair_rows(b, i), :]
            for j in range(i, blocks):
                taken = product(factor, block_ref[pair_rows(b, j), :], ((0,), (0,)))
                block_ref[pair_rows(i, j), :] = block_ref[pair_rows(i, j), :] - taken
            for j in range(b):
                taken = product(factor, side_ref[pair_rows(j, b), :], ((0,), (0,)))
                side_ref[pair_rows(j, i), :] = side_ref[pair_rows(j, i), :] - taken
            side_ref[pair_rows(b, i), :] = -product(factor, inverse, ((0,), (0,)))
    for i in range(blocks):
        for j in range(blocks):
            here = (slice(i * BLOCK, (i + 1) * BLOCK), slice(j * BLOCK, (j + 1) * BLOCK))
            upper_out[here] = block_ref[pair_rows(i, j), :] if i <= j else zero
            inverse_out[here] = side_ref[pair_rows(j, i), :] if j <= i else zero
    for i in range(blocks):
        size = (i + 1) * BLOCK
        done_ref[i * BLOCK : size, :] = product(inverse_out[i * BLOCK : size, 0:size], modes_ref[:, 0:size], ((1,), (1,)))


def finish_kernel(packed_ref, snap_ref, upper_ref, inverse_ref, done_ref, basis_ref, factor_ref, cross_ref, corner_ref, back_ref):
    count = snap_ref.shape[0]
    rank = upper_ref.shape[0]
    blocks = rank // BLOCK
    base = blocks // 2 * BLOCK
    for i in range(blocks):
        at, side = (i // 2) * BLOCK, (i % 2) * count
        cross_ref[i * BLOCK : (i + 1) * BLOCK, :] = packed_ref[at : at + BLOCK, side : side + count]
    cross = product(inverse_ref[...], cross_ref[...], ((1,), (0,)))
    rows = count // 8
    corner_ref[...] = jnp.zeros_like(corner_ref)
    corner_ref[:, 0:count] = packed_ref[base : base + count, 0:count] - product(cross, cross, ((0,), (0,)))
    unit = identity(BLOCK)
    main = [corner_ref[8 * i : 8 * i + 8, :] for i in range(rows)]
    side = [unit[8 * i : 8 * i + 8, :] for i in range(rows)]
    eliminate(main, side, corner_ref, back_ref, 0, rows, rows)
    rest = snap_ref[...] - product(cross, done_ref[...], ((0,), (0,)))
    basis_ref[0:rank, :] = done_ref[...]
    basis_ref[rank:, :] = product(back_ref[:, 0:count], rest, ((1,), (0,)))
    factor_ref[0:rank, 0:rank] = upper_ref[...]
    factor_ref[0:rank, rank:] = cross
    factor_ref[rank:, 0:rank] = jnp.zeros((count, rank), jnp.float32)
    factor_ref[rank:, rank:] = corner_ref[:, 0:count]


def f32(*shape):
    return jax.ShapeDtypeStruct(shape, jnp.float32)


def everyones(value, axis):
    copies = jnp.broadcast_to(value[None], (lax.axis_size(axis),) + value.shape)
    return lax.all_to_all(copies, axis, 0, 0, tiled=True)


def sections(velocity, assign, extra):
    comps, depth, across, height = velocity.shape
    before, after = both_ways(velocity[:, :, :WIDE], velocity[:, :, across - WIDE :], "grp", True)
    field = jnp.concatenate([velocity, after, before], axis=2)
    before, after = both_ways(field[:, :WIDE], field[:, depth - WIDE :], "slab", True)
    field = jnp.concatenate([before, field, after], axis=1)
    deep, rows = field.shape[1], field.shape[2]
    where = jnp.stack([lax.axis_index("row"), lax.axis_size("row")]).astype(jnp.int32)
    tiles = -(-comps * deep * WIDE // height)
    edges = vmem_call(pack_kernel, f32(lax.axis_size("row"), tiles, rows, height), [SM, VM], moved=4 * field.size)(where, field)
    edges = lax.all_to_all(edges, "row", 0, 0, tiled=True)
    pieces = comps * across // 2
    wide = (comps, deep, rows, 2 * height)
    return vmem_call(
        sections_kernel,
        [f32(comps, depth, across, height), f32(pieces, 2 * depth + extra, height)],
        [SM, SM, VM, VM],
        scratch=[
            pltpu.VMEM(wide, jnp.float32),
            pltpu.VMEM(wide, jnp.float32),
            pltpu.VMEM((comps, deep, across, height), jnp.float32),
            pltpu.SMEM((pieces,), jnp.int32),
        ],
        moved=32 * field.size,
    )(assign, where, field, edges)


def on_device(velocity, modes, planes, assign):
    count, rank, held = planes.shape[0], modes.shape[1], modes.shape[0]
    groups, slabs = lax.axis_size("grp"), lax.axis_size("slab")
    scale = 1.0 / float(held * groups * slabs * lax.axis_size("row"))
    blocks = rank // BLOCK
    rows = blocks * (blocks + 1) // 2 * BLOCK
    tall = blocks // 2 * BLOCK + count
    part = tall // groups
    each = rows // groups
    piece = -(-each // (8 * slabs)) * 8

    packed = vmem_call(modes_gram_kernel, f32(rows, BLOCK), [VM], flops=12 * held * rank * rank, moved=4 * modes.size)(modes)
    share = lax.psum_scatter(packed, "grp", scatter_dimension=0, tiled=True)
    share = jnp.pad(share, ((0, piece * slabs - each), (0, 0))).reshape(slabs, piece, BLOCK)

    advanced, sent = sections(velocity, assign, piece)
    sent = lax.dynamic_update_slice(sent, share, (0, sent.shape[1] - piece, 0))
    received = lax.all_to_all(sent, "slab", 0, 0, tiled=True)
    both, snap = vmem_call(
        snapshot_gram_kernel,
        [f32(groups, part + piece, BLOCK), f32(count, held)],
        [SM, VM, VM],
        scratch=[pltpu.VMEM((tall, BLOCK), jnp.float32)],
    )(planes, received, modes)
    both = jnp.sum(lax.all_to_all(both, "row", 0, 0, tiled=True), axis=0)
    both = everyones(both, "slab") * scale
    both = jnp.concatenate([jnp.sum(both[:, :part], axis=0), both[:, part:].reshape(-1, BLOCK)[:each]])
    both = everyones(both, "grp")
    share = jnp.sum(both[:, :part], axis=0)
    packed = everyones(share, "row").reshape(tall, BLOCK)

    upper, inverse, done = vmem_call(
        modes_factor_kernel,
        [f32(rank, rank), f32(rank, rank), f32(rank, held)],
        [VM, VM],
        scratch=[pltpu.VMEM((rows, BLOCK), jnp.float32)] * 2 + [pltpu.VMEM((BLOCK, BLOCK), jnp.float32)] * 2,
        flops=28 * 1000 * 1000 * 1000,
    )(both, modes)
    basis, factor = vmem_call(
        finish_kernel,
        [f32(rank + count, held), f32(rank + count, rank + count)],
        [VM, VM, VM, VM, VM],
        scratch=[
            pltpu.VMEM((rank, count), jnp.float32),
            pltpu.VMEM((count, BLOCK), jnp.float32),
            pltpu.VMEM((count, BLOCK), jnp.float32),
        ],
    )(packed, snap, upper, inverse, done)
    return (advanced, basis.T, factor)


def solution(mesh):
    placed = (P(None, "slab", "grp", "row"), P(("grp", "slab", "row"), None), P(), P())
    return jax.shard_map(
        on_device,
        mesh=mesh,
        in_specs=placed,
        out_specs=(P(None, "slab", "grp", "row"), P(("grp", "slab", "row"), None), P()),
        check_vma=False,
    )
```

```python
import functools

import jax
import jax.numpy as jnp
from jax import lax
from jax.experimental import pallas as pl
from jax.experimental.pallas import tpu as pltpu
from jax.sharding import PartitionSpec as P

step_size = 0.05
viscosity = 1.0
third = 1.0 / 3.0
carry_back = -5.0 / 9.0
second_gain = 15.0 / 16.0

ALL = ("grp", "slab", "row")
WIDE = 4
BLOCK = 128
VMEM_LIMIT = 20 * 1024 * 1024


def vmem_call(kernel, out_shape, in_specs, scratch=(), aliases=None, flops=0, moved=0):
    single = not isinstance(out_shape, (list, tuple))
    whole = pl.BlockSpec(memory_space=pltpu.VMEM)
    return pl.pallas_call(
        kernel,
        out_shape=out_shape,
        in_specs=in_specs,
        out_specs=whole if single else [whole] * len(out_shape),
        scratch_shapes=list(scratch),
        input_output_aliases=aliases or {},
        cost_estimate=pl.CostEstimate(flops=flops, bytes_accessed=moved, transcendentals=0),
        compiler_params=pltpu.CompilerParams(vmem_limit_bytes=VMEM_LIMIT),
    )


VM = pl.BlockSpec(memory_space=pltpu.VMEM)
SM = pl.BlockSpec(memory_space=pltpu.SMEM)


def product(left, right, dims):
    return lax.dot_general(
        left,
        right,
        (dims, ((), ())),
        precision=lax.Precision.HIGHEST,
        preferred_element_type=jnp.float32,
    )


def total(terms):
    while len(terms) > 1:
        terms = [a + b for a, b in zip(terms[::2], terms[1::2])] + ([terms[-1]] if len(terms) % 2 else [])
    return terms[0]


def both_ways(low, high, axis, wrap):
    devices = lax.axis_size(axis)
    up = [(i, (i + 1) % devices) for i in range(devices if wrap else devices - 1)]
    down = [(j, i) for i, j in up]
    return lax.ppermute(high, axis, up), lax.ppermute(low, axis, down)


def pack_kernel(row_ref, field_ref, share_ref, out_ref):
    comps, depth, rows, lanes = field_ref.shape
    planes = comps * depth
    group = lanes // WIDE
    lane = lax.broadcasted_iota(jnp.int32, (rows, lanes), 1)
    row, last = row_ref[0], row_ref[1] - 1
    heads, tails = [], []
    tiles = -(-planes // group)
    summed = total([share_ref[g] for g in range(share_ref.shape[0])])
    each = summed.shape[0] // out_ref.shape[0]
    for slot in range(out_ref.shape[0]):
        out_ref[slot, tiles * rows : tiles * rows + each, :] = summed[slot * each : (slot + 1) * each]
    for tile in range(tiles):
        head = jnp.zeros((rows, lanes), jnp.float32)
        tail = jnp.zeros((rows, lanes), jnp.float32)
        for q in range(min(group, planes - tile * group)):
            c, z = divmod(tile * group + q, depth)
            value = field_ref[c, z]
            here = (lane >= WIDE * q) & (lane < WIDE * (q + 1))
            head = jnp.where(here, pltpu.roll(value, (WIDE * q) % lanes, 1), head)
            tail = jnp.where(here, pltpu.roll(value, (WIDE * (q + 1)) % lanes, 1), tail)
        heads.append(head)
        tails.append(tail)

    @pl.when(row > 0)
    def _():
        for tile, head in enumerate(heads):
            out_ref[jnp.maximum(row - 1, 0), tile * rows : (tile + 1) * rows, :] = head

    @pl.when(row < last)
    def _():
        for tile, tail in enumerate(tails):
            out_ref[jnp.minimum(row + 1, last), tile * rows : (tile + 1) * rows, :] = tail


def parts_of(value, axis):
    size = value.shape[axis]
    return [pltpu.roll(value, shift % size, axis) for shift in (2, 1, -1, -2)]


def derivatives(parts, centre):
    first = (parts[0] - parts[3]) + 8.0 * (parts[2] - parts[1])
    second = 16.0 * (parts[1] + parts[2]) - (parts[0] + parts[3])
    return first, second


def sections_kernel(
    assign_ref, row_ref, field_ref, edges_ref, out_ref, sent_ref, wide_ref, mid_ref, q_ref, place_ref
):
    comps, depth_wide, rows, lanes = field_ref.shape
    depth, across = out_ref.shape[1], out_ref.shape[2]
    group = lanes // WIDE
    lane = lax.broadcasted_iota(jnp.int32, (rows, lanes), 1)

    row, last = row_ref[0], row_ref[1] - 1
    previous, following = jnp.maximum(row - 1, 0), jnp.minimum(row + 1, last)
    from_next = (lane < WIDE) & (row < last)
    from_previous = (lane >= lanes - WIDE) & (row > 0)

    for c in range(comps):
        for z in range(depth_wide):
            tile, q = divmod(c * depth_wide + z, group)
            after = pltpu.roll(edges_ref[following, tile * rows : (tile + 1) * rows, :], (-WIDE * q) % lanes, 1)
            before = pltpu.roll(edges_ref[previous, tile * rows : (tile + 1) * rows, :], (-WIDE * (q + 1)) % lanes, 1)
            halo = jnp.where(from_next, after, jnp.where(from_previous, before, 0.0))
            wide_ref[c, z, :, 0:lanes] = field_ref[c, z]
            wide_ref[c, z, :, lanes : 2 * lanes] = halo

    edge = lax.broadcasted_iota(jnp.int32, (rows, 2 * lanes), 1)
    outside = ((edge >= lanes + lanes // 2) & (row == 0)) | ((edge >= lanes) & (edge < lanes + lanes // 2) & (row == last))

    def tendency(speeds, centre, along_z, along_x, along_y):
        dz_first, dz_second = derivatives(along_z, centre)
        dx_first, dx_second = derivatives(along_x, centre)
        dy_first, dy_second = derivatives(along_y, centre)
        convect = speeds[0] * dx_first + speeds[1] * dy_first + speeds[2] * dz_first
        return viscosity * ((dx_second + dy_second) + (dz_second - 90.0 * centre)) - convect

    def first_section(z, _):
        speeds = [wide_ref[c, z] for c in range(comps)]
        for c in range(comps):
            along_z = [wide_ref[c, z + k] for k in (-2, -1, 1, 2)]
            slope = tendency(speeds, speeds[c], along_z, parts_of(speeds[c], 0), parts_of(speeds[c], 1))
            q = (step_size / 12.0) * slope
            mid_ref[c, z] = jnp.where(outside, 0.0, speeds[c] + third * q)
            q_ref[c, z] = q[:across, :lanes]
        return 0

    lax.fori_loop(2, depth_wide - 2, first_section, 0)

    def second_section(z, _):
        speeds = [mid_ref[c, z, 0:across, 0:lanes] for c in range(comps)]
        for c in range(comps):
            along_z = [mid_ref[c, z + k, 0:across, 0:lanes] for k in (-2, -1, 1, 2)]
            along_x = [p[:across] for p in parts_of(mid_ref[c, z, :, 0:lanes], 0)]
            along_y = [p[:, :lanes] for p in parts_of(mid_ref[c, z, 0:across, :], 1)]
            slope = tendency(speeds, speeds[c], along_z, along_x, along_y)
            q = carry_back * q_ref[c, z] + (step_size / 12.0) * slope
            out_ref[c, z - WIDE] = speeds[c] + second_gain * q
        return 0

    lax.fori_loop(WIDE, WIDE + depth, second_section, 0)

    tiles = -(-comps * depth_wide // group)
    each = edges_ref.shape[1] - tiles * rows
    summed = total([edges_ref[r, tiles * rows :, :] for r in range(edges_ref.shape[0])])
    for s in range(sent_ref.shape[0]):
        sent_ref[s, 2 * depth : 2 * depth + each, :] = summed

    pieces = sent_ref.shape[0]
    for s in range(pieces):
        place_ref[assign_ref[s]] = s
    pairs = across // 2
    for b in range(pieces):
        c, x = b // pairs, 2 * (b % pairs)
        to = place_ref[b]
        sent_ref[to, 0:depth, :] = out_ref[c, :, x, :]
        sent_ref[to, depth : 2 * depth, :] = out_ref[c, :, x + 1, :]


def pair_index(i, j):
    return i * 4 - (i * (i - 1)) // 2 + (j - i)


def modes_gram_kernel(modes_ref, out_ref):
    count = modes_ref.shape[1] // BLOCK
    for i in range(count):
        for j in range(i, count):
            at = pair_index(i, j) * BLOCK
            out_ref[at : at + BLOCK, :] = product(
                modes_ref[:, i * BLOCK : (i + 1) * BLOCK], modes_ref[:, j * BLOCK : (j + 1) * BLOCK], ((0,), (0,))
            )


def snapshot_gram_kernel(planes_ref, received_ref, modes_ref, out_ref, snap_ref, packed_ref):
    count, held = snap_ref.shape
    slabs = received_ref.shape[0]
    blocks = modes_ref.shape[1] // BLOCK
    tall = packed_ref.shape[0]
    groups, share = out_ref.shape[0], tall // out_ref.shape[0]
    ours = out_ref.shape[1] - share
    depth = (received_ref.shape[1] - ours) // 2
    for k in range(count):
        slab, z = planes_ref[k] // depth, planes_ref[k] % depth
        snap_ref[k : k + 1, 0:BLOCK] = received_ref[slab, pl.ds(z, 1), :]
        snap_ref[k : k + 1, BLOCK:held] = received_ref[slab, pl.ds(z + depth, 1), :]
    snap = snap_ref[...]
    cross = product(modes_ref[...], snap, ((0,), (1,)))
    for b in range(blocks):
        at, side = (b // 2) * BLOCK, (b % 2) * count
        packed_ref[at : at + BLOCK, side : side + count] = cross[b * BLOCK : (b + 1) * BLOCK, :]
    base = blocks // 2 * BLOCK
    packed_ref[base : base + count, :] = jnp.zeros((count, BLOCK), jnp.float32)
    packed_ref[base : base + count, 0:count] = product(snap, snap, ((1,), (1,)))
    summed = total([received_ref[s, 2 * depth :, :] for s in range(slabs)])
    for g in range(groups):
        out_ref[g, 0:share, :] = packed_ref[g * share : (g + 1) * share, :]
        out_ref[g, share:, :] = summed


def merge_kernel(scale, part, received_ref, out_ref):
    slots = received_ref.shape[0]
    each = (out_ref.shape[1] - part) // slots
    summed = total([received_ref[r, 0:part, :] for r in range(slots)]) * scale
    rows = [received_ref[r, part : part + each, :] * scale for r in range(slots)]
    whole = jnp.concatenate([summed] + rows, axis=0)
    for g in range(out_ref.shape[0]):
        out_ref[g] = whole


def lanes_of(value, j):
    return jnp.broadcast_to(value[:, j : j + 1], value.shape)


def row_of(value, i):
    return jnp.broadcast_to(value[i : i + 1, :], value.shape)


def eliminate(main, side, upper_ref, inverse_ref, rows):
    sub = lax.broadcasted_iota(jnp.int32, (8, BLOCK), 0)
    lane = lax.broadcasted_iota(jnp.int32, (8, BLOCK), 1)
    for p in range(rows):
        top, left = main[p], side[p]
        columns = [lanes_of(top, 8 * p + j) for j in range(8)]
        a = [[row_of(columns[j], i) if j <= i else None for j in range(8)] for i in range(8)]
        upper = [row_of(top, j) for j in range(8)]
        lower = [row_of(left, j) for j in range(8)]
        v = [[None] * 8 for _ in range(8)]
        for j in range(8):
            scale = lax.rsqrt(a[j][j])
            below = {i: a[i][j] * scale for i in range(j + 1, 8)}
            for m in range(j + 1, 8):
                for i in range(m, 8):
                    a[i][m] = a[i][m] - below[i] * below[m]
            upper[j], lower[j] = upper[j] * scale, lower[j] * scale
            v[j][j] = scale
            for k in range(j):
                v[j][k] = v[j][k] * scale
            for m in range(j + 1, 8):
                upper[m] = upper[m] - below[m] * upper[j]
                lower[m] = lower[m] - below[m] * lower[j]
                for k in range(j + 1):
                    taken = below[m] * v[j][k]
                    v[m][k] = -taken if v[m][k] is None else v[m][k] - taken
        factor, inverse = upper[7], lower[7]
        for j in range(7):
            factor = jnp.where(sub == j, upper[j], factor)
            inverse = jnp.where(sub == j, lower[j], inverse)
        upper_ref[8 * p : 8 * p + 8, :] = jnp.where(lane >= 8 * p + sub, factor, 0.0)
        inverse_ref[8 * p : 8 * p + 8, :] = inverse
        if p + 1 == rows:
            break
        top_rows = [total([v[i][j] * upper[i] for i in range(j, 8)]) for j in range(8)]
        left_rows = [total([v[i][j] * lower[i] for i in range(j, 8)]) for j in range(8)]
        for i in range(p + 1, rows):
            here = [lanes_of(main[i], 8 * p + j) for j in range(8)]
            main[i] = main[i] - total([here[j] * top_rows[j] for j in range(8)])
            side[i] = side[i] - total([here[j] * left_rows[j] for j in range(8)])


def identity(size):
    lane = lax.broadcasted_iota(jnp.int32, (size, size), 1)
    sub = lax.broadcasted_iota(jnp.int32, (size, size), 0)
    return jnp.where(lane == sub, 1.0, 0.0)


def pair_rows(i, j):
    at = pair_index(i, j) * BLOCK
    return slice(at, at + BLOCK)


def modes_factor_kernel(gathered_ref, modes_ref, upper_out, inverse_out, done_ref, block_ref, side_ref, upper_ref, inverse_ref):
    blocks = modes_ref.shape[1] // BLOCK
    groups = gathered_ref.shape[0]
    each = block_ref.shape[0] // groups
    rows = BLOCK // 8
    lane = lax.broadcasted_iota(jnp.int32, (BLOCK, BLOCK), 1)
    sub = lax.broadcasted_iota(jnp.int32, (BLOCK, BLOCK), 0)
    unit = identity(BLOCK)
    zero = jnp.zeros((BLOCK, BLOCK), jnp.float32)
    for g in range(groups):
        block_ref[g * each : (g + 1) * each, :] = gathered_ref[g, gathered_ref.shape[1] - each :, :]
    for b in range(blocks):
        value = block_ref[pair_rows(b, b), :]
        value = jnp.where(lane >= sub, value, value.T)
        main = [value[8 * i : 8 * i + 8, :] for i in range(rows)]
        side = [unit[8 * i : 8 * i + 8, :] for i in range(rows)]
        eliminate(main, side, upper_ref, inverse_ref, rows)
        inverse = inverse_ref[...]
        block_ref[pair_rows(b, b), :] = upper_ref[...]
        side_ref[pair_rows(b, b), :] = inverse
        for j in range(b):
            side_ref[pair_rows(j, b), :] = product(inverse, side_ref[pair_rows(j, b), :], ((1,), (0,)))
        for j in range(b + 1, blocks):
            block_ref[pair_rows(b, j), :] = product(inverse, block_ref[pair_rows(b, j), :], ((1,), (0,)))
        for i in range(b + 1, blocks):
            factor = block_ref[pair_rows(b, i), :]
            for j in range(i, blocks):
                taken = product(factor, block_ref[pair_rows(b, j), :], ((0,), (0,)))
                block_ref[pair_rows(i, j), :] = block_ref[pair_rows(i, j), :] - taken
            for j in range(b):
                taken = product(factor, side_ref[pair_rows(j, b), :], ((0,), (0,)))
                side_ref[pair_rows(j, i), :] = side_ref[pair_rows(j, i), :] - taken
            side_ref[pair_rows(b, i), :] = -product(factor, inverse, ((0,), (0,)))
    for i in range(blocks):
        for j in range(blocks):
            here = (slice(i * BLOCK, (i + 1) * BLOCK), slice(j * BLOCK, (j + 1) * BLOCK))
            upper_out[here] = block_ref[pair_rows(i, j), :] if i <= j else zero
            inverse_out[here] = side_ref[pair_rows(j, i), :] if j <= i else zero
    for i in range(blocks):
        size = (i + 1) * BLOCK
        done_ref[i * BLOCK : size, :] = product(inverse_out[i * BLOCK : size, 0:size], modes_ref[:, 0:size], ((1,), (1,)))


def finish_kernel(packed_ref, snap_ref, upper_ref, inverse_ref, done_ref, basis_ref, factor_ref, cross_ref, corner_ref, back_ref):
    count = snap_ref.shape[0]
    rank = upper_ref.shape[0]
    blocks = rank // BLOCK
    base = blocks // 2 * BLOCK
    for i in range(blocks):
        at, side = (i // 2) * BLOCK, (i % 2) * count
        cross_ref[i * BLOCK : (i + 1) * BLOCK, :] = packed_ref[at : at + BLOCK, side : side + count]
    cross = product(inverse_ref[...], cross_ref[...], ((1,), (0,)))
    rows = count // 8
    corner_ref[...] = jnp.zeros_like(corner_ref)
    corner_ref[:, 0:count] = packed_ref[base : base + count, 0:count] - product(cross, cross, ((0,), (0,)))
    unit = identity(BLOCK)
    main = [corner_ref[8 * i : 8 * i + 8, :] for i in range(rows)]
    side = [unit[8 * i : 8 * i + 8, :] for i in range(rows)]
    eliminate(main, side, corner_ref, back_ref, rows)
    rest = snap_ref[...] - product(cross, done_ref[...], ((0,), (0,)))
    basis_ref[0:rank, :] = done_ref[...]
    basis_ref[rank:, :] = product(back_ref[:, 0:count], rest, ((1,), (0,)))
    factor_ref[0:rank, 0:rank] = upper_ref[...]
    factor_ref[0:rank, rank:] = cross
    factor_ref[rank:, 0:rank] = jnp.zeros((count, rank), jnp.float32)
    factor_ref[rank:, rank:] = corner_ref[:, 0:count]


def f32(*shape):
    return jax.ShapeDtypeStruct(shape, jnp.float32)


def everyones(value, axis):
    copies = jnp.broadcast_to(value[None], (lax.axis_size(axis),) + value.shape)
    return lax.all_to_all(copies, axis, 0, 0, tiled=True)


def sections(velocity, assign, shares):
    comps, depth, across, height = velocity.shape
    before, after = both_ways(velocity[:, :, :WIDE], velocity[:, :, across - WIDE :], "grp", True)
    before, after, shares = lax.optimization_barrier((before, after, shares))
    field = jnp.concatenate([velocity, after, before], axis=2)
    before, after = both_ways(field[:, :WIDE], field[:, depth - WIDE :], "slab", True)
    field = jnp.concatenate([before, field, after], axis=1)
    deep, rows = field.shape[1], field.shape[2]
    places = lax.axis_size("row")
    each = shares.shape[1] // places
    where = jnp.stack([lax.axis_index("row"), places]).astype(jnp.int32)
    tiles = -(-comps * deep * WIDE // height)
    edges = vmem_call(pack_kernel, f32(places, tiles * rows + each, height), [SM, VM, VM], moved=4 * field.size)(
        where, field, shares
    )
    edges = lax.all_to_all(edges, "row", 0, 0, tiled=True)
    pieces = comps * across // 2
    wide = (comps, deep, rows, 2 * height)
    return vmem_call(
        sections_kernel,
        [f32(comps, depth, across, height), f32(pieces, 2 * depth + each, height)],
        [SM, SM, VM, VM],
        scratch=[
            pltpu.VMEM(wide, jnp.float32),
            pltpu.VMEM(wide, jnp.float32),
            pltpu.VMEM((comps, deep, across, height), jnp.float32),
            pltpu.SMEM((pieces,), jnp.int32),
        ],
        moved=32 * field.size,
    )(assign, where, field, edges)


def on_device(velocity, modes, planes, assign):
    count, rank, held = planes.shape[0], modes.shape[1], modes.shape[0]
    groups, slabs, places = lax.axis_size("grp"), lax.axis_size("slab"), lax.axis_size("row")
    scale = 1.0 / float(held * groups * slabs * places)
    blocks = rank // BLOCK
    rows = blocks * (blocks + 1) // 2 * BLOCK
    tall = blocks // 2 * BLOCK + count
    part = tall // places

    packed = vmem_call(modes_gram_kernel, f32(rows, BLOCK), [VM], flops=12 * held * rank * rank, moved=4 * modes.size)(modes)
    shares = lax.all_to_all(packed.reshape(groups, -1, BLOCK), "grp", 0, 0, tiled=True)
    advanced, sent = sections(velocity, assign, shares)
    received = lax.all_to_all(sent, "slab", 0, 0, tiled=True)
    each = rows // groups // places
    both, snap = vmem_call(
        snapshot_gram_kernel,
        [f32(places, part + each, BLOCK), f32(count, held)],
        [SM, VM, VM],
        scratch=[pltpu.VMEM((tall, BLOCK), jnp.float32)],
    )(planes, received, modes)
    both = lax.all_to_all(both, "row", 0, 0, tiled=True)
    both = vmem_call(functools.partial(merge_kernel, scale, part), f32(groups, part + rows // groups, BLOCK), [VM])(both)
    both = lax.all_to_all(both, "grp", 0, 0, tiled=True)
    share = everyones(jnp.sum(both[:, :part], axis=0), "slab")

    upper, inverse, done = vmem_call(
        modes_factor_kernel,
        [f32(rank, rank), f32(rank, rank), f32(rank, held)],
        [VM, VM],
        scratch=[pltpu.VMEM((rows, BLOCK), jnp.float32)] * 2 + [pltpu.VMEM((BLOCK, BLOCK), jnp.float32)] * 2,
        flops=20 * 1000 * 1000 * 1000,
    )(both, modes)
    share, upper = lax.optimization_barrier((share, upper))
    packed = everyones(jnp.sum(share, axis=0), "row").reshape(tall, BLOCK)
    basis, factor = vmem_call(
        finish_kernel,
        [f32(rank + count, held), f32(rank + count, rank + count)],
        [VM, VM, VM, VM, VM],
        scratch=[
            pltpu.VMEM((rank, count), jnp.float32),
            pltpu.VMEM((count, BLOCK), jnp.float32),
            pltpu.VMEM((count, BLOCK), jnp.float32),
        ],
    )(packed, snap, upper, inverse, done)
    return (advanced, basis.T, factor)


def solution(mesh):
    placed = (P(None, "slab", "grp", "row"), P(("grp", "slab", "row"), None), P(), P())
    return jax.shard_map(
        on_device,
        mesh=mesh,
        in_specs=placed,
        out_specs=(P(None, "slab", "grp", "row"), P(("grp", "slab", "row"), None), P()),
        check_vma=False,
    )
```

```python
import functools

import jax
import jax.numpy as jnp
from jax import lax
from jax.experimental import pallas as pl
from jax.experimental.pallas import tpu as pltpu
from jax.sharding import PartitionSpec as P

step_size = 0.05
viscosity = 1.0
third = 1.0 / 3.0
carry_back = -5.0 / 9.0
second_gain = 15.0 / 16.0

ALL = ("grp", "slab", "row")
WIDE = 4
BLOCK = 128
VMEM_LIMIT = 20 * 1024 * 1024


def vmem_call(kernel, out_shape, in_specs, scratch=(), aliases=None, flops=0, moved=0):
    single = not isinstance(out_shape, (list, tuple))
    whole = pl.BlockSpec(memory_space=pltpu.VMEM)
    return pl.pallas_call(
        kernel,
        out_shape=out_shape,
        in_specs=in_specs,
        out_specs=whole if single else [whole] * len(out_shape),
        scratch_shapes=list(scratch),
        input_output_aliases=aliases or {},
        cost_estimate=pl.CostEstimate(flops=flops, bytes_accessed=moved, transcendentals=0),
        compiler_params=pltpu.CompilerParams(vmem_limit_bytes=VMEM_LIMIT),
    )


VM = pl.BlockSpec(memory_space=pltpu.VMEM)
SM = pl.BlockSpec(memory_space=pltpu.SMEM)


def product(left, right, dims):
    return lax.dot_general(
        left,
        right,
        (dims, ((), ())),
        precision=lax.Precision.HIGHEST,
        preferred_element_type=jnp.float32,
    )


def total(terms):
    while len(terms) > 1:
        terms = [a + b for a, b in zip(terms[::2], terms[1::2])] + ([terms[-1]] if len(terms) % 2 else [])
    return terms[0]


def both_ways(low, high, axis, wrap):
    devices = lax.axis_size(axis)
    up = [(i, (i + 1) % devices) for i in range(devices if wrap else devices - 1)]
    down = [(j, i) for i, j in up]
    return lax.ppermute(high, axis, up), lax.ppermute(low, axis, down)


def pack_kernel(row_ref, field_ref, share_ref, out_ref):
    comps, depth, rows, lanes = field_ref.shape
    planes = comps * depth
    group = lanes // WIDE
    lane = lax.broadcasted_iota(jnp.int32, (rows, lanes), 1)
    row, last = row_ref[0], row_ref[1] - 1
    heads, tails = [], []
    tiles = -(-planes // group)
    summed = total([share_ref[g] for g in range(share_ref.shape[0])])
    each = summed.shape[0] // out_ref.shape[0]
    for slot in range(out_ref.shape[0]):
        out_ref[slot, tiles * rows : tiles * rows + each, :] = summed[slot * each : (slot + 1) * each]
    for tile in range(tiles):
        head = jnp.zeros((rows, lanes), jnp.float32)
        tail = jnp.zeros((rows, lanes), jnp.float32)
        for q in range(min(group, planes - tile * group)):
            c, z = divmod(tile * group + q, depth)
            value = field_ref[c, z]
            here = (lane >= WIDE * q) & (lane < WIDE * (q + 1))
            head = jnp.where(here, pltpu.roll(value, (WIDE * q) % lanes, 1), head)
            tail = jnp.where(here, pltpu.roll(value, (WIDE * (q + 1)) % lanes, 1), tail)
        heads.append(head)
        tails.append(tail)

    @pl.when(row > 0)
    def _():
        for tile, head in enumerate(heads):
            out_ref[jnp.maximum(row - 1, 0), tile * rows : (tile + 1) * rows, :] = head

    @pl.when(row < last)
    def _():
        for tile, tail in enumerate(tails):
            out_ref[jnp.minimum(row + 1, last), tile * rows : (tile + 1) * rows, :] = tail


def parts_of(value, axis):
    size = value.shape[axis]
    return [pltpu.roll(value, shift % size, axis) for shift in (2, 1, -1, -2)]


def derivatives(parts, centre):
    first = (parts[0] - parts[3]) + 8.0 * (parts[2] - parts[1])
    second = 16.0 * (parts[1] + parts[2]) - (parts[0] + parts[3])
    return first, second


def planes_each(section, first, last, unroll):
    while (last - first) % unroll:
        unroll -= 1

    def step(i, _):
        for k in range(unroll):
            section(first + i * unroll + k)
        return 0

    lax.fori_loop(0, (last - first) // unroll, step, 0)


def sections_kernel(
    assign_ref, row_ref, field_ref, edges_ref, out_ref, sent_ref, wide_ref, mid_ref, q_ref, place_ref
):
    comps, depth_wide, rows, lanes = field_ref.shape
    depth, across = out_ref.shape[1], out_ref.shape[2]
    group = lanes // WIDE
    lane = lax.broadcasted_iota(jnp.int32, (rows, lanes), 1)

    row, last = row_ref[0], row_ref[1] - 1
    previous, following = jnp.maximum(row - 1, 0), jnp.minimum(row + 1, last)
    from_next = (lane < WIDE) & (row < last)
    from_previous = (lane >= lanes - WIDE) & (row > 0)

    for c in range(comps):
        for z in range(depth_wide):
            tile, q = divmod(c * depth_wide + z, group)
            after = pltpu.roll(edges_ref[following, tile * rows : (tile + 1) * rows, :], (-WIDE * q) % lanes, 1)
            before = pltpu.roll(edges_ref[previous, tile * rows : (tile + 1) * rows, :], (-WIDE * (q + 1)) % lanes, 1)
            halo = jnp.where(from_next, after, jnp.where(from_previous, before, 0.0))
            wide_ref[c, z, :, 0:lanes] = field_ref[c, z]
            wide_ref[c, z, :, lanes : 2 * lanes] = halo

    edge = lax.broadcasted_iota(jnp.int32, (rows, 2 * lanes), 1)
    outside = ((edge >= lanes + lanes // 2) & (row == 0)) | ((edge >= lanes) & (edge < lanes + lanes // 2) & (row == last))

    def tendency(speeds, centre, along_z, along_x, along_y):
        dz_first, dz_second = derivatives(along_z, centre)
        dx_first, dx_second = derivatives(along_x, centre)
        dy_first, dy_second = derivatives(along_y, centre)
        convect = speeds[0] * dx_first + speeds[1] * dy_first + speeds[2] * dz_first
        return viscosity * ((dx_second + dy_second) + (dz_second - 90.0 * centre)) - convect

    def first_section(z):
        speeds = [wide_ref[c, z] for c in range(comps)]
        for c in range(comps):
            along_z = [wide_ref[c, z + k] for k in (-2, -1, 1, 2)]
            slope = tendency(speeds, speeds[c], along_z, parts_of(speeds[c], 0), parts_of(speeds[c], 1))
            q = (step_size / 12.0) * slope
            mid_ref[c, z] = jnp.where(outside, 0.0, speeds[c] + third * q)
            q_ref[c, z] = q[:across, :lanes]

    planes_each(first_section, 2, depth_wide - 2, 3)

    def second_section(z):
        speeds = [mid_ref[c, z, 0:across, 0:lanes] for c in range(comps)]
        for c in range(comps):
            along_z = [mid_ref[c, z + k, 0:across, 0:lanes] for k in (-2, -1, 1, 2)]
            along_x = [p[:across] for p in parts_of(mid_ref[c, z, :, 0:lanes], 0)]
            along_y = [p[:, :lanes] for p in parts_of(mid_ref[c, z, 0:across, :], 1)]
            slope = tendency(speeds, speeds[c], along_z, along_x, along_y)
            q = carry_back * q_ref[c, z] + (step_size / 12.0) * slope
            out_ref[c, z - WIDE] = speeds[c] + second_gain * q

    planes_each(second_section, WIDE, WIDE + depth, 8)

    tiles = -(-comps * depth_wide // group)
    each = edges_ref.shape[1] - tiles * rows
    summed = total([edges_ref[r, tiles * rows :, :] for r in range(edges_ref.shape[0])])
    for s in range(sent_ref.shape[0]):
        sent_ref[s, 2 * depth : 2 * depth + each, :] = summed

    pieces = sent_ref.shape[0]
    for s in range(pieces):
        place_ref[assign_ref[s]] = s
    pairs = across // 2
    for b in range(pieces):
        c, x = b // pairs, 2 * (b % pairs)
        to = place_ref[b]
        sent_ref[to, 0:depth, :] = out_ref[c, :, x, :]
        sent_ref[to, depth : 2 * depth, :] = out_ref[c, :, x + 1, :]


def pair_index(i, j):
    return i * 4 - (i * (i - 1)) // 2 + (j - i)


def modes_gram_kernel(modes_ref, out_ref):
    count = modes_ref.shape[1] // BLOCK
    for i in range(count):
        for j in range(i, count):
            at = pair_index(i, j) * BLOCK
            out_ref[at : at + BLOCK, :] = product(
                modes_ref[:, i * BLOCK : (i + 1) * BLOCK], modes_ref[:, j * BLOCK : (j + 1) * BLOCK], ((0,), (0,))
            )


def snapshot_gram_kernel(planes_ref, received_ref, modes_ref, out_ref, snap_ref, packed_ref):
    count, held = snap_ref.shape
    slabs = received_ref.shape[0]
    blocks = modes_ref.shape[1] // BLOCK
    tall = packed_ref.shape[0]
    groups, share = out_ref.shape[0], tall // out_ref.shape[0]
    ours = out_ref.shape[1] - share
    depth = (received_ref.shape[1] - ours) // 2
    for k in range(count):
        slab, z = planes_ref[k] // depth, planes_ref[k] % depth
        snap_ref[k : k + 1, 0:BLOCK] = received_ref[slab, pl.ds(z, 1), :]
        snap_ref[k : k + 1, BLOCK:held] = received_ref[slab, pl.ds(z + depth, 1), :]
    snap = snap_ref[...]
    cross = product(modes_ref[...], snap, ((0,), (1,)))
    for b in range(blocks):
        at, side = (b // 2) * BLOCK, (b % 2) * count
        packed_ref[at : at + BLOCK, side : side + count] = cross[b * BLOCK : (b + 1) * BLOCK, :]
    base = blocks // 2 * BLOCK
    packed_ref[base : base + count, :] = jnp.zeros((count, BLOCK), jnp.float32)
    packed_ref[base : base + count, 0:count] = product(snap, snap, ((1,), (1,)))
    summed = total([received_ref[s, 2 * depth :, :] for s in range(slabs)])
    for g in range(groups):
        out_ref[g, 0:share, :] = packed_ref[g * share : (g + 1) * share, :]
        out_ref[g, share:, :] = summed


def merge_kernel(scale, part, received_ref, out_ref):
    slots = received_ref.shape[0]
    each = (out_ref.shape[1] - part) // slots
    summed = total([received_ref[r, 0:part, :] for r in range(slots)]) * scale
    rows = [received_ref[r, part : part + each, :] * scale for r in range(slots)]
    whole = jnp.concatenate([summed] + rows, axis=0)
    for g in range(out_ref.shape[0]):
        out_ref[g] = whole


def lanes_of(value, j):
    return jnp.broadcast_to(value[:, j : j + 1], value.shape)


def row_of(value, i):
    return jnp.broadcast_to(value[i : i + 1, :], value.shape)


def eliminate(main, side, upper_ref, inverse_ref, rows):
    sub = lax.broadcasted_iota(jnp.int32, (8, BLOCK), 0)
    lane = lax.broadcasted_iota(jnp.int32, (8, BLOCK), 1)
    for p in range(rows):
        top, left = main[p], side[p]
        columns = [lanes_of(top, 8 * p + j) for j in range(8)]
        a = [[row_of(columns[j], i) if j <= i else None for j in range(8)] for i in range(8)]
        upper = [row_of(top, j) for j in range(8)]
        lower = [row_of(left, j) for j in range(8)]
        v = [[None] * 8 for _ in range(8)]
        for j in range(8):
            scale = lax.rsqrt(a[j][j])
            below = {i: a[i][j] * scale for i in range(j + 1, 8)}
            for m in range(j + 1, 8):
                for i in range(m, 8):
                    a[i][m] = a[i][m] - below[i] * below[m]
            upper[j], lower[j] = upper[j] * scale, lower[j] * scale
            v[j][j] = scale
            for k in range(j):
                v[j][k] = v[j][k] * scale
            for m in range(j + 1, 8):
                upper[m] = upper[m] - below[m] * upper[j]
                lower[m] = lower[m] - below[m] * lower[j]
                for k in range(j + 1):
                    taken = below[m] * v[j][k]
                    v[m][k] = -taken if v[m][k] is None else v[m][k] - taken
        factor, inverse = upper[7], lower[7]
        for j in range(7):
            factor = jnp.where(sub == j, upper[j], factor)
            inverse = jnp.where(sub == j, lower[j], inverse)
        upper_ref[8 * p : 8 * p + 8, :] = jnp.where(lane >= 8 * p + sub, factor, 0.0)
        inverse_ref[8 * p : 8 * p + 8, :] = inverse
        if p + 1 == rows:
            break
        top_rows = [total([v[i][j] * upper[i] for i in range(j, 8)]) for j in range(8)]
        left_rows = [total([v[i][j] * lower[i] for i in range(j, 8)]) for j in range(8)]
        for i in range(p + 1, rows):
            here = [lanes_of(main[i], 8 * p + j) for j in range(8)]
            main[i] = main[i] - total([here[j] * top_rows[j] for j in range(8)])
            side[i] = side[i] - total([here[j] * left_rows[j] for j in range(8)])


def identity(size):
    lane = lax.broadcasted_iota(jnp.int32, (size, size), 1)
    sub = lax.broadcasted_iota(jnp.int32, (size, size), 0)
    return jnp.where(lane == sub, 1.0, 0.0)


def pair_rows(i, j):
    at = pair_index(i, j) * BLOCK
    return slice(at, at + BLOCK)


def factor_step(b, blocks, block_ref, side_ref, upper_ref, inverse_ref):
    rows = BLOCK // 8
    lane = lax.broadcasted_iota(jnp.int32, (BLOCK, BLOCK), 1)
    sub = lax.broadcasted_iota(jnp.int32, (BLOCK, BLOCK), 0)
    unit = identity(BLOCK)
    value = block_ref[pair_rows(b, b), :]
    value = jnp.where(lane >= sub, value, value.T)
    main = [value[8 * i : 8 * i + 8, :] for i in range(rows)]
    side = [unit[8 * i : 8 * i + 8, :] for i in range(rows)]
    eliminate(main, side, upper_ref, inverse_ref, rows)
    inverse = inverse_ref[...]
    block_ref[pair_rows(b, b), :] = upper_ref[...]
    side_ref[pair_rows(b, b), :] = inverse
    for j in range(b):
        side_ref[pair_rows(j, b), :] = product(inverse, side_ref[pair_rows(j, b), :], ((1,), (0,)))
    for j in range(b + 1, blocks):
        block_ref[pair_rows(b, j), :] = product(inverse, block_ref[pair_rows(b, j), :], ((1,), (0,)))
    for i in range(b + 1, blocks):
        factor = block_ref[pair_rows(b, i), :]
        for j in range(i, blocks):
            taken = product(factor, block_ref[pair_rows(b, j), :], ((0,), (0,)))
            block_ref[pair_rows(i, j), :] = block_ref[pair_rows(i, j), :] - taken
        for j in range(b):
            taken = product(factor, side_ref[pair_rows(j, b), :], ((0,), (0,)))
            side_ref[pair_rows(j, i), :] = side_ref[pair_rows(j, i), :] - taken
        side_ref[pair_rows(b, i), :] = -product(factor, inverse, ((0,), (0,)))


def first_factor_kernel(steps, blocks, gathered_ref, block_ref, side_ref, upper_ref, inverse_ref):
    groups = gathered_ref.shape[0]
    each = block_ref.shape[0] // groups
    for g in range(groups):
        block_ref[g * each : (g + 1) * each, :] = gathered_ref[g, gathered_ref.shape[1] - each :, :]
    for b in range(steps, blocks):
        for j in range(b, blocks):
            side_ref[pair_rows(b, j), :] = jnp.zeros((BLOCK, BLOCK), jnp.float32)
    for b in range(steps):
        factor_step(b, blocks, block_ref, side_ref, upper_ref, inverse_ref)


def last_factor_kernel(
    steps, block_in, side_in, modes_ref, upper_out, inverse_out, done_ref, block_ref, side_ref, upper_ref, inverse_ref
):
    blocks = modes_ref.shape[1] // BLOCK
    zero = jnp.zeros((BLOCK, BLOCK), jnp.float32)
    block_ref[...] = block_in[...]
    side_ref[...] = side_in[...]
    for b in range(steps, blocks):
        factor_step(b, blocks, block_ref, side_ref, upper_ref, inverse_ref)
    for i in range(blocks):
        for j in range(blocks):
            here = (slice(i * BLOCK, (i + 1) * BLOCK), slice(j * BLOCK, (j + 1) * BLOCK))
            upper_out[here] = block_ref[pair_rows(i, j), :] if i <= j else zero
            inverse_out[here] = side_ref[pair_rows(j, i), :] if j <= i else zero
    for i in range(blocks):
        size = (i + 1) * BLOCK
        done_ref[i * BLOCK : size, :] = product(inverse_out[i * BLOCK : size, 0:size], modes_ref[:, 0:size], ((1,), (1,)))


def finish_kernel(packed_ref, snap_ref, upper_ref, inverse_ref, done_ref, basis_ref, factor_ref, cross_ref, corner_ref, back_ref):
    count = snap_ref.shape[0]
    rank = upper_ref.shape[0]
    blocks = rank // BLOCK
    base = blocks // 2 * BLOCK
    for i in range(blocks):
        at, side = (i // 2) * BLOCK, (i % 2) * count
        cross_ref[i * BLOCK : (i + 1) * BLOCK, :] = packed_ref[at : at + BLOCK, side : side + count]
    cross = product(inverse_ref[...], cross_ref[...], ((1,), (0,)))
    rows = count // 8
    corner_ref[...] = jnp.zeros_like(corner_ref)
    corner_ref[:, 0:count] = packed_ref[base : base + count, 0:count] - product(cross, cross, ((0,), (0,)))
    unit = identity(BLOCK)
    main = [corner_ref[8 * i : 8 * i + 8, :] for i in range(rows)]
    side = [unit[8 * i : 8 * i + 8, :] for i in range(rows)]
    eliminate(main, side, corner_ref, back_ref, rows)
    rest = snap_ref[...] - product(cross, done_ref[...], ((0,), (0,)))
    basis_ref[0:rank, :] = done_ref[...]
    basis_ref[rank:, :] = product(back_ref[:, 0:count], rest, ((1,), (0,)))
    factor_ref[0:rank, 0:rank] = upper_ref[...]
    factor_ref[0:rank, rank:] = cross
    factor_ref[rank:, 0:rank] = jnp.zeros((count, rank), jnp.float32)
    factor_ref[rank:, rank:] = corner_ref[:, 0:count]


def f32(*shape):
    return jax.ShapeDtypeStruct(shape, jnp.float32)


def everyones(value, axis):
    copies = jnp.broadcast_to(value[None], (lax.axis_size(axis),) + value.shape)
    return lax.all_to_all(copies, axis, 0, 0, tiled=True)


def sections(velocity, assign, shares):
    comps, depth, across, height = velocity.shape
    before, after = both_ways(velocity[:, :, :WIDE], velocity[:, :, across - WIDE :], "grp", True)
    before, after, shares = lax.optimization_barrier((before, after, shares))
    field = jnp.concatenate([velocity, after, before], axis=2)
    before, after = both_ways(field[:, :WIDE], field[:, depth - WIDE :], "slab", True)
    field = jnp.concatenate([before, field, after], axis=1)
    deep, rows = field.shape[1], field.shape[2]
    places = lax.axis_size("row")
    each = shares.shape[1] // places
    where = jnp.stack([lax.axis_index("row"), places]).astype(jnp.int32)
    tiles = -(-comps * deep * WIDE // height)
    edges = vmem_call(pack_kernel, f32(places, tiles * rows + each, height), [SM, VM, VM], moved=4 * field.size)(
        where, field, shares
    )
    edges = lax.all_to_all(edges, "row", 0, 0, tiled=True)
    pieces = comps * across // 2
    wide = (comps, deep, rows, 2 * height)
    return vmem_call(
        sections_kernel,
        [f32(comps, depth, across, height), f32(pieces, 2 * depth + each, height)],
        [SM, SM, VM, VM],
        scratch=[
            pltpu.VMEM(wide, jnp.float32),
            pltpu.VMEM(wide, jnp.float32),
            pltpu.VMEM((comps, deep, across, height), jnp.float32),
            pltpu.SMEM((pieces,), jnp.int32),
        ],
        moved=32 * field.size,
    )(assign, where, field, edges)


def on_device(velocity, modes, planes, assign):
    count, rank, held = planes.shape[0], modes.shape[1], modes.shape[0]
    groups, slabs, places = lax.axis_size("grp"), lax.axis_size("slab"), lax.axis_size("row")
    scale = 1.0 / float(held * groups * slabs * places)
    blocks = rank // BLOCK
    rows = blocks * (blocks + 1) // 2 * BLOCK
    tall = blocks // 2 * BLOCK + count
    part = tall // places

    packed = vmem_call(modes_gram_kernel, f32(rows, BLOCK), [VM], flops=12 * held * rank * rank, moved=4 * modes.size)(modes)
    shares = lax.all_to_all(packed.reshape(groups, -1, BLOCK), "grp", 0, 0, tiled=True)
    advanced, sent = sections(velocity, assign, shares)
    received = lax.all_to_all(sent, "slab", 0, 0, tiled=True)
    each = rows // groups // places
    both, snap = vmem_call(
        snapshot_gram_kernel,
        [f32(places, part + each, BLOCK), f32(count, held)],
        [SM, VM, VM],
        scratch=[pltpu.VMEM((tall, BLOCK), jnp.float32)],
    )(planes, received, modes)
    both = lax.all_to_all(both, "row", 0, 0, tiled=True)
    both = vmem_call(functools.partial(merge_kernel, scale, part), f32(groups, part + rows // groups, BLOCK), [VM])(both)
    both = lax.all_to_all(both, "grp", 0, 0, tiled=True)
    share = everyones(jnp.sum(both[:, :part], axis=0), "slab")

    steps = blocks // 2
    pair = [pltpu.VMEM((BLOCK, BLOCK), jnp.float32)] * 2
    cost = 10 * 1000 * 1000 * 1000
    lower = vmem_call(
        functools.partial(first_factor_kernel, steps, blocks), [f32(rows, BLOCK)] * 2, [VM], scratch=pair, flops=cost
    )(both)
    share, *lower = lax.optimization_barrier((share, *lower))
    packed = everyones(jnp.sum(share, axis=0), "row").reshape(tall, BLOCK)
    upper, inverse, done = vmem_call(
        functools.partial(last_factor_kernel, steps),
        [f32(rank, rank), f32(rank, rank), f32(rank, held)],
        [VM, VM, VM],
        scratch=[pltpu.VMEM((rows, BLOCK), jnp.float32)] * 2 + pair,
        flops=cost,
    )(*lower, modes)
    basis, factor = vmem_call(
        finish_kernel,
        [f32(rank + count, held), f32(rank + count, rank + count)],
        [VM, VM, VM, VM, VM],
        scratch=[
            pltpu.VMEM((rank, count), jnp.float32),
            pltpu.VMEM((count, BLOCK), jnp.float32),
            pltpu.VMEM((count, BLOCK), jnp.float32),
        ],
    )(packed, snap, upper, inverse, done)
    return (advanced, basis.T, factor)


def solution(mesh):
    placed = (P(None, "slab", "grp", "row"), P(("grp", "slab", "row"), None), P(), P())
    return jax.shard_map(
        on_device,
        mesh=mesh,
        in_specs=placed,
        out_specs=(P(None, "slab", "grp", "row"), P(("grp", "slab", "row"), None), P()),
        check_vma=False,
    )
```

```python
import functools

import jax
import jax.numpy as jnp
from jax import lax
from jax.experimental import pallas as pl
from jax.experimental.pallas import tpu as pltpu
from jax.sharding import PartitionSpec as P

step_size = 0.05
viscosity = 1.0
third = 1.0 / 3.0
carry_back = -5.0 / 9.0
second_gain = 15.0 / 16.0

ALL = ("grp", "slab", "row")
WIDE = 4
BLOCK = 128
VMEM_LIMIT = 20 * 1024 * 1024


def vmem_call(kernel, out_shape, in_specs, scratch=(), aliases=None, flops=0, moved=0):
    single = not isinstance(out_shape, (list, tuple))
    whole = pl.BlockSpec(memory_space=pltpu.VMEM)
    return pl.pallas_call(
        kernel,
        out_shape=out_shape,
        in_specs=in_specs,
        out_specs=whole if single else [whole] * len(out_shape),
        scratch_shapes=list(scratch),
        input_output_aliases=aliases or {},
        cost_estimate=pl.CostEstimate(flops=flops, bytes_accessed=moved, transcendentals=0),
        compiler_params=pltpu.CompilerParams(vmem_limit_bytes=VMEM_LIMIT),
    )


VM = pl.BlockSpec(memory_space=pltpu.VMEM)
SM = pl.BlockSpec(memory_space=pltpu.SMEM)


def product(left, right, dims):
    return lax.dot_general(
        left,
        right,
        (dims, ((), ())),
        precision=lax.Precision.HIGHEST,
        preferred_element_type=jnp.float32,
    )


def total(terms):
    while len(terms) > 1:
        terms = [a + b for a, b in zip(terms[::2], terms[1::2])] + ([terms[-1]] if len(terms) % 2 else [])
    return terms[0]


def both_ways(low, high, axis, wrap):
    devices = lax.axis_size(axis)
    up = [(i, (i + 1) % devices) for i in range(devices if wrap else devices - 1)]
    down = [(j, i) for i, j in up]
    return lax.ppermute(high, axis, up), lax.ppermute(low, axis, down)


def pack_kernel(row_ref, field_ref, share_ref, out_ref):
    comps, depth, rows, lanes = field_ref.shape
    planes = comps * depth
    group = lanes // WIDE
    lane = lax.broadcasted_iota(jnp.int32, (rows, lanes), 1)
    row, last = row_ref[0], row_ref[1] - 1
    heads, tails = [], []
    tiles = -(-planes // group)
    summed = total([share_ref[g] for g in range(share_ref.shape[0])])
    each = summed.shape[0] // out_ref.shape[0]
    for slot in range(out_ref.shape[0]):
        out_ref[slot, tiles * rows : tiles * rows + each, :] = summed[slot * each : (slot + 1) * each]
    for tile in range(tiles):
        head = jnp.zeros((rows, lanes), jnp.float32)
        tail = jnp.zeros((rows, lanes), jnp.float32)
        for q in range(min(group, planes - tile * group)):
            c, z = divmod(tile * group + q, depth)
            value = field_ref[c, z]
            here = (lane >= WIDE * q) & (lane < WIDE * (q + 1))
            head = jnp.where(here, pltpu.roll(value, (WIDE * q) % lanes, 1), head)
            tail = jnp.where(here, pltpu.roll(value, (WIDE * (q + 1)) % lanes, 1), tail)
        heads.append(head)
        tails.append(tail)

    @pl.when(row > 0)
    def _():
        for tile, head in enumerate(heads):
            out_ref[jnp.maximum(row - 1, 0), tile * rows : (tile + 1) * rows, :] = head

    @pl.when(row < last)
    def _():
        for tile, tail in enumerate(tails):
            out_ref[jnp.minimum(row + 1, last), tile * rows : (tile + 1) * rows, :] = tail


def parts_of(value, axis):
    size = value.shape[axis]
    return [pltpu.roll(value, shift % size, axis) for shift in (2, 1, -1, -2)]


def derivatives(parts, centre):
    first = (parts[0] - parts[3]) + 8.0 * (parts[2] - parts[1])
    second = 16.0 * (parts[1] + parts[2]) - (parts[0] + parts[3])
    return first, second


def planes_each(section, first, last, unroll):
    while (last - first) % unroll:
        unroll -= 1

    def step(i, _):
        for k in range(unroll):
            section(first + i * unroll + k)
        return 0

    lax.fori_loop(0, (last - first) // unroll, step, 0)


def sections_kernel(
    assign_ref, row_ref, field_ref, edges_ref, out_ref, sent_ref, wide_ref, mid_ref, q_ref, place_ref
):
    comps, depth_wide, rows, lanes = field_ref.shape
    depth, across = out_ref.shape[1], out_ref.shape[2]
    group = lanes // WIDE
    lane = lax.broadcasted_iota(jnp.int32, (rows, lanes), 1)

    row, last = row_ref[0], row_ref[1] - 1
    previous, following = jnp.maximum(row - 1, 0), jnp.minimum(row + 1, last)
    from_next = (lane < WIDE) & (row < last)
    from_previous = (lane >= lanes - WIDE) & (row > 0)

    for c in range(comps):
        for z in range(depth_wide):
            tile, q = divmod(c * depth_wide + z, group)
            after = pltpu.roll(edges_ref[following, tile * rows : (tile + 1) * rows, :], (-WIDE * q) % lanes, 1)
            before = pltpu.roll(edges_ref[previous, tile * rows : (tile + 1) * rows, :], (-WIDE * (q + 1)) % lanes, 1)
            halo = jnp.where(from_next, after, jnp.where(from_previous, before, 0.0))
            wide_ref[c, z, :, 0:lanes] = field_ref[c, z]
            wide_ref[c, z, :, lanes : 2 * lanes] = halo

    edge = lax.broadcasted_iota(jnp.int32, (rows, 2 * lanes), 1)
    outside = ((edge >= lanes + lanes // 2) & (row == 0)) | ((edge >= lanes) & (edge < lanes + lanes // 2) & (row == last))

    def tendency(speeds, centre, along_z, along_x, along_y):
        dz_first, dz_second = derivatives(along_z, centre)
        dx_first, dx_second = derivatives(along_x, centre)
        dy_first, dy_second = derivatives(along_y, centre)
        convect = speeds[0] * dx_first + speeds[1] * dy_first + speeds[2] * dz_first
        return viscosity * ((dx_second + dy_second) + (dz_second - 90.0 * centre)) - convect

    def first_section(z):
        speeds = [wide_ref[c, z] for c in range(comps)]
        for c in range(comps):
            along_z = [wide_ref[c, z + k] for k in (-2, -1, 1, 2)]
            slope = tendency(speeds, speeds[c], along_z, parts_of(speeds[c], 0), parts_of(speeds[c], 1))
            q = (step_size / 12.0) * slope
            mid_ref[c, z] = jnp.where(outside, 0.0, speeds[c] + third * q)
            q_ref[c, z] = q[:across, :lanes]

    planes_each(first_section, 2, depth_wide - 2, 6)

    def second_section(z):
        speeds = [mid_ref[c, z, 0:across, 0:lanes] for c in range(comps)]
        for c in range(comps):
            along_z = [mid_ref[c, z + k, 0:across, 0:lanes] for k in (-2, -1, 1, 2)]
            along_x = [p[:across] for p in parts_of(mid_ref[c, z, :, 0:lanes], 0)]
            along_y = [p[:, :lanes] for p in parts_of(mid_ref[c, z, 0:across, :], 1)]
            slope = tendency(speeds, speeds[c], along_z, along_x, along_y)
            q = carry_back * q_ref[c, z] + (step_size / 12.0) * slope
            out_ref[c, z - WIDE] = speeds[c] + second_gain * q

    planes_each(second_section, WIDE, WIDE + depth, 16)

    tiles = -(-comps * depth_wide // group)
    each = edges_ref.shape[1] - tiles * rows
    summed = total([edges_ref[r, tiles * rows :, :] for r in range(edges_ref.shape[0])])
    for s in range(sent_ref.shape[0]):
        sent_ref[s, 2 * depth : 2 * depth + each, :] = summed

    pieces = sent_ref.shape[0]
    for s in range(pieces):
        place_ref[assign_ref[s]] = s
    pairs = across // 2
    for b in range(pieces):
        c, x = b // pairs, 2 * (b % pairs)
        to = place_ref[b]
        sent_ref[to, 0:depth, :] = out_ref[c, :, x, :]
        sent_ref[to, depth : 2 * depth, :] = out_ref[c, :, x + 1, :]


def pair_index(i, j):
    return i * 4 - (i * (i - 1)) // 2 + (j - i)


def modes_gram_kernel(modes_ref, out_ref):
    count = modes_ref.shape[1] // BLOCK
    for i in range(count):
        for j in range(i, count):
            at = pair_index(i, j) * BLOCK
            out_ref[at : at + BLOCK, :] = product(
                modes_ref[:, i * BLOCK : (i + 1) * BLOCK], modes_ref[:, j * BLOCK : (j + 1) * BLOCK], ((0,), (0,))
            )


def snapshot_gram_kernel(planes_ref, received_ref, modes_ref, out_ref, snap_ref, packed_ref):
    count, held = snap_ref.shape
    slabs = received_ref.shape[0]
    blocks = modes_ref.shape[1] // BLOCK
    tall = packed_ref.shape[0]
    groups, share = out_ref.shape[0], tall // out_ref.shape[0]
    ours = out_ref.shape[1] - share
    depth = (received_ref.shape[1] - ours) // 2
    for k in range(count):
        slab, z = planes_ref[k] // depth, planes_ref[k] % depth
        snap_ref[k : k + 1, 0:BLOCK] = received_ref[slab, pl.ds(z, 1), :]
        snap_ref[k : k + 1, BLOCK:held] = received_ref[slab, pl.ds(z + depth, 1), :]
    snap = snap_ref[...]
    cross = product(modes_ref[...], snap, ((0,), (1,)))
    for b in range(blocks):
        at, side = (b // 2) * BLOCK, (b % 2) * count
        packed_ref[at : at + BLOCK, side : side + count] = cross[b * BLOCK : (b + 1) * BLOCK, :]
    base = blocks // 2 * BLOCK
    packed_ref[base : base + count, :] = jnp.zeros((count, BLOCK), jnp.float32)
    packed_ref[base : base + count, 0:count] = product(snap, snap, ((1,), (1,)))
    summed = total([received_ref[s, 2 * depth :, :] for s in range(slabs)])
    for g in range(groups):
        out_ref[g, 0:share, :] = packed_ref[g * share : (g + 1) * share, :]
        out_ref[g, share:, :] = summed


def merge_kernel(scale, part, received_ref, out_ref):
    slots = received_ref.shape[0]
    each = (out_ref.shape[1] - part) // slots
    summed = total([received_ref[r, 0:part, :] for r in range(slots)]) * scale
    rows = [received_ref[r, part : part + each, :] * scale for r in range(slots)]
    whole = jnp.concatenate([summed] + rows, axis=0)
    for g in range(out_ref.shape[0]):
        out_ref[g] = whole


def lanes_of(value, j):
    return jnp.broadcast_to(value[:, j : j + 1], value.shape)


def row_of(value, i):
    return jnp.broadcast_to(value[i : i + 1, :], value.shape)


def eliminate(main, side, upper_ref, inverse_ref, rows):
    sub = lax.broadcasted_iota(jnp.int32, (8, BLOCK), 0)
    lane = lax.broadcasted_iota(jnp.int32, (8, BLOCK), 1)
    for p in range(rows):
        top, left = main[p], side[p]
        columns = [lanes_of(top, 8 * p + j) for j in range(8)]
        a = [[row_of(columns[j], i) if j <= i else None for j in range(8)] for i in range(8)]
        upper = [row_of(top, j) for j in range(8)]
        lower = [row_of(left, j) for j in range(8)]
        v = [[None] * 8 for _ in range(8)]
        for j in range(8):
            scale = lax.rsqrt(a[j][j])
            below = {i: a[i][j] * scale for i in range(j + 1, 8)}
            for m in range(j + 1, 8):
                for i in range(m, 8):
                    a[i][m] = a[i][m] - below[i] * below[m]
            upper[j], lower[j] = upper[j] * scale, lower[j] * scale
            v[j][j] = scale
            for k in range(j):
                v[j][k] = v[j][k] * scale
            for m in range(j + 1, 8):
                upper[m] = upper[m] - below[m] * upper[j]
                lower[m] = lower[m] - below[m] * lower[j]
                for k in range(j + 1):
                    taken = below[m] * v[j][k]
                    v[m][k] = -taken if v[m][k] is None else v[m][k] - taken
        factor, inverse = upper[7], lower[7]
        for j in range(7):
            factor = jnp.where(sub == j, upper[j], factor)
            inverse = jnp.where(sub == j, lower[j], inverse)
        upper_ref[8 * p : 8 * p + 8, :] = jnp.where(lane >= 8 * p + sub, factor, 0.0)
        inverse_ref[8 * p : 8 * p + 8, :] = inverse
        if p + 1 == rows:
            break
        top_rows = [total([v[i][j] * upper[i] for i in range(j, 8)]) for j in range(8)]
        left_rows = [total([v[i][j] * lower[i] for i in range(j, 8)]) for j in range(8)]
        for i in range(p + 1, rows):
            here = [lanes_of(main[i], 8 * p + j) for j in range(8)]
            main[i] = main[i] - total([here[j] * top_rows[j] for j in range(8)])
            side[i] = side[i] - total([here[j] * left_rows[j] for j in range(8)])


def identity(size):
    lane = lax.broadcasted_iota(jnp.int32, (size, size), 1)
    sub = lax.broadcasted_iota(jnp.int32, (size, size), 0)
    return jnp.where(lane == sub, 1.0, 0.0)


def pair_rows(i, j):
    at = pair_index(i, j) * BLOCK
    return slice(at, at + BLOCK)


def factor_step(b, blocks, block_ref, side_ref, upper_ref, inverse_ref):
    rows = BLOCK // 8
    lane = lax.broadcasted_iota(jnp.int32, (BLOCK, BLOCK), 1)
    sub = lax.broadcasted_iota(jnp.int32, (BLOCK, BLOCK), 0)
    unit = identity(BLOCK)
    value = block_ref[pair_rows(b, b), :]
    value = jnp.where(lane >= sub, value, value.T)
    main = [value[8 * i : 8 * i + 8, :] for i in range(rows)]
    side = [unit[8 * i : 8 * i + 8, :] for i in range(rows)]
    eliminate(main, side, upper_ref, inverse_ref, rows)
    inverse = inverse_ref[...]
    block_ref[pair_rows(b, b), :] = upper_ref[...]
    side_ref[pair_rows(b, b), :] = inverse
    for j in range(b):
        side_ref[pair_rows(j, b), :] = product(inverse, side_ref[pair_rows(j, b), :], ((1,), (0,)))
    for j in range(b + 1, blocks):
        block_ref[pair_rows(b, j), :] = product(inverse, block_ref[pair_rows(b, j), :], ((1,), (0,)))
    for i in range(b + 1, blocks):
        factor = block_ref[pair_rows(b, i), :]
        for j in range(i, blocks):
            taken = product(factor, block_ref[pair_rows(b, j), :], ((0,), (0,)))
            block_ref[pair_rows(i, j), :] = block_ref[pair_rows(i, j), :] - taken
        for j in range(b):
            taken = product(factor, side_ref[pair_rows(j, b), :], ((0,), (0,)))
            side_ref[pair_rows(j, i), :] = side_ref[pair_rows(j, i), :] - taken
        side_ref[pair_rows(b, i), :] = -product(factor, inverse, ((0,), (0,)))


def first_factor_kernel(steps, blocks, gathered_ref, block_ref, side_ref, upper_ref, inverse_ref):
    groups = gathered_ref.shape[0]
    each = block_ref.shape[0] // groups
    for g in range(groups):
        block_ref[g * each : (g + 1) * each, :] = gathered_ref[g, gathered_ref.shape[1] - each :, :]
    for b in range(steps):
        factor_step(b, blocks, block_ref, side_ref, upper_ref, inverse_ref)


def last_factor_kernel(
    steps, block_in, side_in, modes_ref, upper_out, inverse_out, done_ref, block_ref, side_ref, upper_ref, inverse_ref
):
    blocks = modes_ref.shape[1] // BLOCK
    zero = jnp.zeros((BLOCK, BLOCK), jnp.float32)
    block_ref[...] = block_in[...]
    side_ref[0 : side_in.shape[0], :] = side_in[...]
    for b in range(steps, blocks):
        factor_step(b, blocks, block_ref, side_ref, upper_ref, inverse_ref)
    for i in range(blocks):
        for j in range(blocks):
            here = (slice(i * BLOCK, (i + 1) * BLOCK), slice(j * BLOCK, (j + 1) * BLOCK))
            upper_out[here] = block_ref[pair_rows(i, j), :] if i <= j else zero
            inverse_out[here] = side_ref[pair_rows(j, i), :] if j <= i else zero
    for i in range(blocks):
        size = (i + 1) * BLOCK
        done_ref[i * BLOCK : size, :] = product(inverse_out[i * BLOCK : size, 0:size], modes_ref[:, 0:size], ((1,), (1,)))


def finish_kernel(packed_ref, snap_ref, upper_ref, inverse_ref, done_ref, basis_ref, factor_ref, cross_ref, corner_ref, back_ref):
    count = snap_ref.shape[0]
    rank = upper_ref.shape[0]
    blocks = rank // BLOCK
    base = blocks // 2 * BLOCK
    for i in range(blocks):
        at, side = (i // 2) * BLOCK, (i % 2) * count
        cross_ref[i * BLOCK : (i + 1) * BLOCK, :] = packed_ref[at : at + BLOCK, side : side + count]
    cross = product(inverse_ref[...], cross_ref[...], ((1,), (0,)))
    rows = count // 8
    corner_ref[...] = jnp.zeros_like(corner_ref)
    corner_ref[:, 0:count] = packed_ref[base : base + count, 0:count] - product(cross, cross, ((0,), (0,)))
    unit = identity(BLOCK)
    main = [corner_ref[8 * i : 8 * i + 8, :] for i in range(rows)]
    side = [unit[8 * i : 8 * i + 8, :] for i in range(rows)]
    eliminate(main, side, corner_ref, back_ref, rows)
    rest = snap_ref[...] - product(cross, done_ref[...], ((0,), (0,)))
    basis_ref[0:rank, :] = done_ref[...]
    basis_ref[rank:, :] = product(back_ref[:, 0:count], rest, ((1,), (0,)))
    factor_ref[0:rank, 0:rank] = upper_ref[...]
    factor_ref[0:rank, rank:] = cross
    factor_ref[rank:, 0:rank] = jnp.zeros((count, rank), jnp.float32)
    factor_ref[rank:, rank:] = corner_ref[:, 0:count]


def f32(*shape):
    return jax.ShapeDtypeStruct(shape, jnp.float32)


def everyones(value, axis):
    copies = jnp.broadcast_to(value[None], (lax.axis_size(axis),) + value.shape)
    return lax.all_to_all(copies, axis, 0, 0, tiled=True)


def sections(velocity, assign, shares):
    comps, depth, across, height = velocity.shape
    before, after = both_ways(velocity[:, :, :WIDE], velocity[:, :, across - WIDE :], "grp", True)
    before, after, shares = lax.optimization_barrier((before, after, shares))
    field = jnp.concatenate([velocity, after, before], axis=2)
    before, after = both_ways(field[:, :WIDE], field[:, depth - WIDE :], "slab", True)
    field = jnp.concatenate([before, field, after], axis=1)
    deep, rows = field.shape[1], field.shape[2]
    places = lax.axis_size("row")
    each = shares.shape[1] // places
    where = jnp.stack([lax.axis_index("row"), places]).astype(jnp.int32)
    tiles = -(-comps * deep * WIDE // height)
    edges = vmem_call(pack_kernel, f32(places, tiles * rows + each, height), [SM, VM, VM], moved=4 * field.size)(
        where, field, shares
    )
    edges = lax.all_to_all(edges, "row", 0, 0, tiled=True)
    pieces = comps * across // 2
    wide = (comps, deep, rows, 2 * height)
    return vmem_call(
        sections_kernel,
        [f32(comps, depth, across, height), f32(pieces, 2 * depth + each, height)],
        [SM, SM, VM, VM],
        scratch=[
            pltpu.VMEM(wide, jnp.float32),
            pltpu.VMEM(wide, jnp.float32),
            pltpu.VMEM((comps, deep, across, height), jnp.float32),
            pltpu.SMEM((pieces,), jnp.int32),
        ],
        moved=32 * field.size,
    )(assign, where, field, edges)


def on_device(velocity, modes, planes, assign):
    count, rank, held = planes.shape[0], modes.shape[1], modes.shape[0]
    groups, slabs, places = lax.axis_size("grp"), lax.axis_size("slab"), lax.axis_size("row")
    scale = 1.0 / float(held * groups * slabs * places)
    blocks = rank // BLOCK
    rows = blocks * (blocks + 1) // 2 * BLOCK
    tall = blocks // 2 * BLOCK + count
    part = tall // places

    packed = vmem_call(modes_gram_kernel, f32(rows, BLOCK), [VM], flops=12 * held * rank * rank, moved=4 * modes.size)(modes)
    shares = lax.all_to_all(packed.reshape(groups, -1, BLOCK), "grp", 0, 0, tiled=True)
    advanced, sent = sections(velocity, assign, shares)
    received = lax.all_to_all(sent, "slab", 0, 0, tiled=True)
    each = rows // groups // places
    both, snap = vmem_call(
        snapshot_gram_kernel,
        [f32(places, part + each, BLOCK), f32(count, held)],
        [SM, VM, VM],
        scratch=[pltpu.VMEM((tall, BLOCK), jnp.float32)],
    )(planes, received, modes)
    both = lax.all_to_all(both, "row", 0, 0, tiled=True)
    both = vmem_call(functools.partial(merge_kernel, scale, part), f32(groups, part + rows // groups, BLOCK), [VM])(both)
    both = lax.all_to_all(both, "grp", 0, 0, tiled=True)
    share = everyones(jnp.sum(both[:, :part], axis=0), "slab")

    steps = blocks // 2
    pair = [pltpu.VMEM((BLOCK, BLOCK), jnp.float32)] * 2
    cost = 10 * 1000 * 1000 * 1000
    lower = vmem_call(
        functools.partial(first_factor_kernel, steps, blocks),
        [f32(rows, BLOCK), f32(pair_index(steps, steps) * BLOCK, BLOCK)],
        [VM],
        scratch=pair,
        flops=cost,
    )(both)
    share, *lower = lax.optimization_barrier((share, *lower))
    packed = everyones(jnp.sum(share, axis=0), "row").reshape(tall, BLOCK)
    upper, inverse, done = vmem_call(
        functools.partial(last_factor_kernel, steps),
        [f32(rank, rank), f32(rank, rank), f32(rank, held)],
        [VM, VM, VM],
        scratch=[pltpu.VMEM((rows, BLOCK), jnp.float32)] * 2 + pair,
        flops=cost,
    )(*lower, modes)
    basis, factor = vmem_call(
        finish_kernel,
        [f32(rank + count, held), f32(rank + count, rank + count)],
        [VM, VM, VM, VM, VM],
        scratch=[
            pltpu.VMEM((rank, count), jnp.float32),
            pltpu.VMEM((count, BLOCK), jnp.float32),
            pltpu.VMEM((count, BLOCK), jnp.float32),
        ],
    )(packed, snap, upper, inverse, done)
    return (advanced, basis.T, factor)


def solution(mesh):
    placed = (P(None, "slab", "grp", "row"), P(("grp", "slab", "row"), None), P(), P())
    return jax.shard_map(
        on_device,
        mesh=mesh,
        in_specs=placed,
        out_specs=(P(None, "slab", "grp", "row"), P(("grp", "slab", "row"), None), P()),
        check_vma=False,
    )
```
